512 devices in a mesh: cell: 128 (over z, y, core), pool: 4 (over x).
Axes of the slice: x: 4, y: 8, z: 8, core: 2. Of those that a mesh axis runs over, the one named last changes fastest.
Arguments:
- fractions: bfloat16 [256, 131072], P(None, 'cell'), may hold values from 0 to 1, as said below
- order: int32 [131072], P('cell'), may hold values from 0 to 131071, as said below
- density: float32 [8, 16, 131072], P('pool', None, 'cell'), may hold values from 0.2 to 5
- area: float32 [16, 131072], P(None, 'cell'), may hold values from 0.05 to 3
- harvest: float32 [8], P('pool'), may hold values from 0.05 to 0.6
Outputs:
- new_density: float32 [8, 16, 131072], P('pool', None, 'cell')
- area_cum: float32 [16, 131072], P(None, 'cell')
- stock_mean: float32 [8, 16], P('pool')
- removed: float32 [16], replicated
The draws below stay inside these ranges and needn't reach their ends.
Inputs may be any that keep to these rules, and one draw needn't show every extreme that they name: A permutation of the cells; of the cells that one device holds in region order, every gridcell block of 1024 positions receives the same number. `fractions`: each column of a cell's matrix sums to one before rounding, with diagonal entries of 0.4 or more.
All inputs are finite; a program needn't handle non-finite values.
Results may differ from the reference program's by a relative error of at most 0.0003.
Values may be sent and summed in bfloat16 or wider, within the bound.
A program may use at most 64 MiB of HBM per device.

```python
import math
import jax
import jax.numpy as jnp
from jax import lax

PFT = 16
POOLS = 8
CELL_DEV = 1024
CELLS = 131072


def draw_fractions(key, part):
    spread = jax.random.uniform(key, (16, 16, CELLS), jnp.float32, 0.0, 0.04)
    ident = jnp.eye(16, dtype=jnp.float32)[:, :, None]
    spread = spread * (1.0 - ident)
    keeping = 1.0 - jnp.sum(spread, axis=0, keepdims=True)
    whole = spread + ident * keeping
    return whole.reshape(256, CELLS).astype(jnp.bfloat16)


def draw_order(key, part):
    blocks = CELLS // CELL_DEV
    slots = CELL_DEV // blocks
    sources = jnp.arange(blocks)
    row_slot = jax.vmap(lambda s: jax.random.permutation(jax.random.fold_in(key, s), CELL_DEV))(sources)
    places = jax.vmap(lambda d: jax.random.permutation(jax.random.fold_in(key, blocks + d), CELL_DEV))(sources)
    target = row_slot // slots
    within = row_slot % slots
    position = target * CELL_DEV + places[target, sources[:, None] * slots + within]
    return position.reshape(CELLS).astype(jnp.int32)


def draw_area(key, part):
    blocks = CELLS // CELL_DEV
    base = jnp.exp(jax.random.uniform(key, (16, CELLS), jnp.float32, jnp.log(0.05), 0.0))
    rising = 1.0 + 2.0 * (jnp.arange(CELLS) // CELL_DEV).astype(jnp.float32) / max(blocks - 1, 1)
    return (base * rising[None]).astype(jnp.float32)


def level_of(own_key, dims, split, low, high):
    factor_of = 1.0
    for dim, shards_of in split:
        heights = jax.random.uniform(jax.random.fold_in(jax.random.fold_in(own_key, 6), dim), (shards_of,), jnp.float32, low / len(split), high / len(split))
        factor_of = factor_of * jnp.repeat(jnp.exp(heights), dims[dim] // shards_of).reshape((-1,) + (1,) * (len(dims) - 1 - dim))
    return factor_of


def setup_inputs(seed: int = 0) -> dict:
    splits = jax.random.split(jax.random.key(seed), 6)
    return {
        "fractions": draw_fractions(jax.random.fold_in(splits[5], 71), 0),
        "order": draw_order(jax.random.fold_in(splits[5], 71), 0),
        "density": jnp.clip(jnp.exp(math.log(5.0) - 3.218876 * jax.random.uniform(splits[2], (POOLS, PFT, CELLS), jnp.float32) ** level_of(splits[2], (POOLS, PFT, CELLS), ((0, 4), (2, 128)), -0.2, 0.2)), 0.2, 5.0),
        "area": draw_area(jax.random.fold_in(splits[5], 71), 0),
        "harvest": jnp.clip(jnp.exp(math.log(0.6) - 2.4849067 * jax.random.uniform(splits[4], (POOLS,), jnp.float32) ** level_of(splits[4], (POOLS,), ((0, 4),), -0.2, 0.2)), 0.05, 0.6),
    }


def transition(block_frac, density, area, harvest):
    matrix = block_frac.astype(jnp.float32).reshape(16, 16, -1)
    stock = area[None] * density
    total = jnp.einsum('ijc,pjc->pic', matrix, stock, precision=lax.Precision.HIGHEST)
    staying = block_frac.astype(jnp.float32)[::17]
    moved = total - staying[None] * stock
    new_stock = staying[None] * stock + (1.0 - harvest[:, None, None]) * moved
    new_area = jnp.einsum('ijc,jc->ic', matrix, area, precision=lax.Precision.HIGHEST)
    new_density = new_stock / new_area[None]
    area_cum = jnp.cumsum(new_area, axis=0) / jnp.sum(new_area, axis=0, keepdims=True)
    stock_sums = jnp.sum(new_stock, axis=2)
    removed_sums = jnp.sum(harvest[:, None, None] * moved, axis=(0, 2))
    return new_density, area_cum, stock_sums, removed_sums


def reference(fractions, order, density, area, harvest):
    block_frac = jnp.zeros_like(fractions).at[:, order].set(fractions)
    new_density, area_cum, stock_sums, removed_sums = transition(block_frac, density, area, harvest)
    return new_density, area_cum, stock_sums / CELLS, removed_sums / CELLS
```

```python
import functools

import jax
import jax.numpy as jnp
from jax import lax
from jax.experimental import pallas as pl
from jax.experimental.pallas import tpu as pltpu
from jax.sharding import Mesh
from jax.sharding import PartitionSpec as P

MESH = pl.DeviceIdType.MESH
F32, BF16, I32 = jnp.float32, jnp.bfloat16, jnp.int32
TYPES = 16


def nt(a, b):
    return lax.dot_general(a, b, (((1,), (1,)), ((), ())), preferred_element_type=F32)


def iota(shape, dim):
    return lax.broadcasted_iota(I32, shape, dim)


def kernel(dims, frac, order, dens, area, harv, out_dens, out_cum, out_mean, out_rem,
           f2, ordv, areav, hsm, hs, hg, dg, stock, oh, psend, pa, ps2, pb, sd, av, bv,
           mv, snd, snd_a, rcv, rcv_a, red0, red1, red2, red3, red4, red5, lsem,
           d_s, d_r, h_s, h_r, p1_s, p1_r, s1_s, s1_r, p2_s, p2_r, s2_s, s2_r,
           o_s, o_r, a_s, a_r, r1_s, r1_r, r2_s, r2_r, r3_s, r3_r):
    nz, ny, nc, nx, cells = dims
    ns = nz * nc
    rank_n = 128 // ns
    half_n = rank_n // 2
    owned = 128 * ny
    rows = 256 // nx
    il_n = TYPES // nx
    pools = 2 * nx
    z, y, c, x = (lax.axis_index(a) for a in ("z", "y", "core", "pool"))
    me = z * nc + c

    def dev_s(o):
        t = lax.rem(me + o, ns)
        return t, (t // nc, y, lax.rem(t, nc), x)

    def dev_y(o):
        t = lax.rem(y + o, ny)
        return t, (z, t, c, x)

    def dev_x(o):
        t = lax.rem(x + o, nx)
        return t, (z, y, c, t)

    local = [
        pltpu.make_async_copy(order, ordv, lsem.at[0]),
        pltpu.make_async_copy(frac.at[pl.ds(pl.multiple_of(x * rows, rows), rows), :], f2.at[pl.ds(0, rows), :], lsem.at[1]),
        pltpu.make_async_copy(frac.at[pl.ds(pl.multiple_of(x * rows, rows), rows), :], f2.at[pl.ds(rows, rows), :], lsem.at[2]),
        pltpu.make_async_copy(area, areav, lsem.at[3]),
        pltpu.make_async_copy(dens, dg.at[pl.ds(2 * x, 2)], lsem.at[4]),
    ]
    for cp in local:
        cp.start()

    barrier = pltpu.get_barrier_semaphore()
    peers = [dev_x(o)[1] for o in range(1, nx)]
    peers += [dev_y(o)[1] for o in range(1, ny)]
    peers += [dev_s(o)[1] for o in range(1, ns)]
    for p in peers:
        pl.semaphore_signal(barrier, inc=1, device_id=p, device_id_type=MESH)

    row8 = iota((8, 128), 0)
    lane8 = iota((8, 128), 1)
    hval = jnp.where(row8 == 2 * x, harv[0], jnp.where(row8 == 2 * x + 1, harv[1], 0.0))
    hs[...] = hval

    local[0].wait()
    ordr = ordv[...]
    dest = ordr // owned
    pos = lax.rem(ordr, owned)
    dz, dy, dc = dest // (ny * nc), lax.rem(dest // nc, ny), lax.rem(dest, nc)
    group = (dz * nc + dc) * ny + dy
    groups = ns * ny
    upper = (iota((128, 128), 0) < iota((128, 128), 1)).astype(BF16)
    ones = jnp.ones((128, 128), BF16)
    before = jnp.zeros((groups, 128), F32)
    ranks = []
    for b in range(ny):
        hot = iota((groups, 128), 0) == group[b:b + 1, :]
        hotb = hot.astype(BF16)
        oh[:, b * 128:(b + 1) * 128] = hotb
        count = jnp.dot(hotb, upper, preferred_element_type=F32) + before
        if b < ny - 1:
            before = before + jnp.dot(hotb, ones, preferred_element_type=F32)
        ranks.append(jnp.sum(jnp.where(hot, count, 0.0), axis=0, keepdims=True))
    rank = jnp.concatenate(ranks, axis=0).astype(I32)
    part = rank // half_n
    sub = lax.rem(rank, half_n)

    lane_of = part * (ns * half_n) + me * half_n + sub
    hi = (pos // 32).astype(F32)
    lo = lax.rem(pos, 32).astype(F32)
    acc_hi = jnp.zeros((groups, 128), F32)
    acc_lo = jnp.zeros((groups, 128), F32)
    for b in range(ny):
        hot = oh[:, b * 128:(b + 1) * 128]
        sel = iota((128, 128), 0) == lane_of[b:b + 1, :]
        acc_hi += nt(hot, jnp.where(sel, hi[b:b + 1, :], 0.0).astype(BF16))
        acc_lo += nt(hot, jnp.where(sel, lo[b:b + 1, :], 0.0).astype(BF16))
    psend[...] = (acc_hi * 32.0 + acc_lo).reshape(ns, ny, 128)

    pl.semaphore_wait(barrier, len(peers))

    sends = []

    def send(src, dst, ss, rs, to):
        cp = pltpu.make_async_remote_copy(src_ref=src, dst_ref=dst, send_sem=ss, recv_sem=rs,
                                          device_id=to, device_id_type=MESH)
        cp.start()
        sends.append(cp)
        return cp

    far_s = sorted(range(1, ns), key=lambda o: -min(o, ns - o))
    far_y = sorted(range(1, ny), key=lambda o: -min(o, ny - o))
    far_x = sorted(range(1, nx), key=lambda o: -min(o, nx - o))

    p1 = []
    for o in far_s:
        t, to = dev_s(o)
        p1.append(send(psend.at[t], pa.at[me], p1_s.at[o], p1_r.at[o], to))

    key = group * half_n + sub
    rho = groups * half_n
    local[1].wait()
    local[2].wait()
    halves = []
    for h in range(2):
        keyh = jnp.where(part == h, key, -1)
        hots = [(iota((rho, 128), 0) == keyh[b:b + 1, :]).astype(BF16) for b in range(ny)]
        halves.append(nt(jnp.concatenate(hots, axis=1), f2[...]))
    lanes = iota((rho, 128), 1)
    moved_cols = jnp.where(lanes < rows, halves[0], halves[1]).astype(BF16)
    sd[...] = moved_cols.reshape(ns, ny, half_n, 128)

    s1 = []
    for o in far_s:
        t, to = dev_s(o)
        s1.append(send(sd.at[t], av.at[me], s1_s.at[o], s1_r.at[o], to))
    av[pl.ds(me, 1)] = sd[pl.ds(me, 1)]
    pa[pl.ds(me, 1)] = psend[pl.ds(me, 1)]

    dcp, hcp = [], []
    for o in far_x:
        t, to = dev_x(o)
        hcp.append(send(hs, hg.at[x], h_s.at[o], h_r.at[o], to))
        dcp.append(send(dens, dg.at[pl.ds(2 * x, 2)], d_s.at[o], d_r.at[o], to))
    hg[pl.ds(x, 1)] = hs[...].reshape(1, 8, 128)

    for cp in p1:
        cp.wait_recv()
    ptot = pa[0]
    for s in range(1, ns):
        ptot = ptot + pa[s]
    ps2[...] = ptot.reshape(ny, 1, 128)
    p2 = []
    for o in far_y:
        t, to = dev_y(o)
        p2.append(send(ps2.at[t], pb.at[y], p2_s.at[o], p2_r.at[o], to))
    pb[pl.ds(y, 1)] = ps2[pl.ds(y, 1)]

    for cp in s1:
        cp.wait_recv()
    s2 = []
    for o in far_y:
        t, to = dev_y(o)
        s2.append(send(av.at[:, t], bv.at[y], s2_s.at[o], s2_r.at[o], to))
    bv[pl.ds(y, 1)] = av[:, pl.ds(y, 1)].reshape(1, ns, half_n, 128)

    for cp in hcp:
        cp.wait_recv()
    harvest = hg[0]
    for s in range(1, nx):
        harvest = harvest + hg[s]
    local[3].wait()
    local[4].wait()
    for cp in dcp:
        cp.wait_recv()
    for j in range(TYPES):
        stock[j] = dg[:, j, :] * areav[j:j + 1, :]

    for cp in p2:
        cp.wait_recv()
    low = iota((1, 128), 1) < 64
    hots = [[], []]
    for q in range(ny // 2):
        a, b = pb[2 * q], pb[2 * q + 1]
        ra, rb = pltpu.roll(a, 64, 1), pltpu.roll(b, 64, 1)
        for h, v in enumerate((jnp.where(low, a, rb), jnp.where(low, ra, b))):
            hots[h].append((iota((owned, 128), 0) == v.astype(I32)).astype(BF16))
    spread = [jnp.concatenate(v, axis=1) for v in hots]

    for cp in s2:
        cp.wait_recv()
    turned = bv[...].reshape(ny * ns * half_n, 128).T
    mv[...] = nt(turned[:rows], spread[0]) + nt(turned[rows:], spread[1])

    keep = 1.0 - harvest
    zero = jnp.zeros((8, 128), F32)

    def block(lb, carry):
        sums, gone = carry
        cols = pl.ds(pl.multiple_of(lb * 128, 128), 128)
        new_sums, new_gone = [], []
        for il in range(il_n):
            tot, na, stay = zero, zero, zero
            for j in range(TYPES):
                m = jnp.broadcast_to(mv[il * TYPES + j:il * TYPES + j + 1, cols], (8, 128))
                term = m * stock[j, :, cols]
                tot = tot + term
                if j % il_n == il:
                    stay = jnp.where(x == j // il_n, term, stay)
                na = na + m * jnp.broadcast_to(areav[j:j + 1, cols], (8, 128))
            moved = tot - stay
            ns_i = stay + keep * moved
            new_sums.append(sums[il] + ns_i)
            new_gone.append(gone[il] + harvest * moved)
            snd[:, il, cols] = ns_i / na
            snd_a[il:il + 1, cols] = na[0:1]
        return tuple(new_sums), tuple(new_gone)

    zeros = (zero,) * il_n
    sums, gone = lax.fori_loop(0, ny, block, (zeros, zeros))

    ocp = []
    for o in far_x:
        t, to = dev_x(o)
        ocp.append(send(snd_a, rcv_a.at[x], a_s.at[o], a_r.at[o], to))
        ocp.append(send(snd.at[pl.ds(2 * t, 2)], rcv.at[x], o_s.at[o], o_r.at[o], to))

    word = zero
    for il in range(il_n):
        i = il_n * x + il
        word = jnp.where(lane8 == i, jnp.sum(sums[il], axis=1, keepdims=True), word)
        word = jnp.where(lane8 == TYPES + i, jnp.sum(gone[il], axis=1, keepdims=True), word)
    red0[...] = word
    rc = []
    for o in far_s:
        t, to = dev_s(o)
        rc.append(send(red0, red1.at[me], r1_s.at[o], r1_r.at[o], to))
    red1[pl.ds(me, 1)] = word.reshape(1, 8, 128)
    rcv[pl.ds(x, 1)] = snd[pl.ds(2 * x, 2)].reshape(1, 2, il_n, owned)
    rcv_a[pl.ds(x, 1)] = snd_a[...].reshape(1, il_n, owned)
    for cp in rc:
        cp.wait_recv()
    tot = red1[0]
    for s in range(1, ns):
        tot = tot + red1[s]
    red2[...] = tot
    rc = []
    for o in far_y:
        t, to = dev_y(o)
        rc.append(send(red2, red3.at[y], r2_s.at[o], r2_r.at[o], to))
    red3[pl.ds(y, 1)] = tot.reshape(1, 8, 128)

    for cp in ocp:
        cp.wait_recv()
    run = None
    for i in range(TYPES):
        xs, il = i // il_n, i % il_n
        r = rcv_a[xs, il:il + 1, :]
        run = r if run is None else run + r
        out_cum[i:i + 1, :] = run
        for q in range(2):
            out_dens[q, i:i + 1, :] = rcv[xs, q, il:il + 1, :]
    out_cum[...] = out_cum[...] / run

    for cp in rc:
        cp.wait_recv()
    tot = red3[0]
    for s in range(1, ny):
        tot = tot + red3[s]
    red4[...] = tot
    rc = []
    for o in far_x:
        t, to = dev_x(o)
        rc.append(send(red4, red5.at[x], r3_s.at[o], r3_r.at[o], to))
    red5[pl.ds(x, 1)] = tot.reshape(1, 8, 128)
    for cp in rc:
        cp.wait_recv()
    tot = red5[0]
    for s in range(1, nx):
        tot = tot + red5[s]
    tot = tot / cells
    red4_out = tot
    red0_out = jnp.sum(pltpu.roll(tot, 128 - TYPES, 1), axis=0, keepdims=True)
    out_rem[...] = red0_out[:, :TYPES]
    hs_pick = jnp.zeros((2, 128), F32)
    for q in range(2):
        pick = jnp.sum(jnp.where(row8 == 2 * x + q, red4_out, 0.0), axis=0, keepdims=True)
        hs_pick = jnp.where(iota((2, 128), 0) == q, pick, hs_pick)
    out_mean[...] = hs_pick[:, :TYPES]
    for cp in sends:
        cp.wait_send()


def solution(mesh):
    nx = mesh.shape["pool"]
    nc = 2
    ncell = mesh.shape["cell"]
    nz = ny = int(round((ncell // nc) ** 0.5))
    finer = Mesh(mesh.devices.reshape(nz, ny, nc, nx), ("z", "y", "core", "pool"))
    ns = nz * nc
    half_n = 64 // ns
    owned = 128 * ny
    rows = 256 // nx
    il_n = TYPES // nx
    groups = ns * ny
    dims = (nz, ny, nc, nx, float(ncell * owned))
    any_, vm = pl.BlockSpec(memory_space=pl.ANY), pl.BlockSpec(memory_space=pltpu.VMEM)
    sm = pl.BlockSpec(memory_space=pltpu.SMEM)
    dma = pltpu.SemaphoreType.DMA

    def body(fractions, order, density, area, harvest):
        scratch = [
            pltpu.VMEM((2 * rows, owned), BF16),
            pltpu.VMEM((ny, 128), I32),
            pltpu.VMEM((TYPES, owned), F32),
            pltpu.SMEM((2,), F32),
            pltpu.VMEM((8, 128), F32),
            pltpu.VMEM((nx, 8, 128), F32),
            pltpu.VMEM((2 * nx, TYPES, owned), F32),
            pltpu.VMEM((TYPES, 2 * nx, owned), F32),
            pltpu.VMEM((groups, owned), BF16),
            pltpu.VMEM((ns, ny, 128), F32),
            pltpu.VMEM((ns, ny, 128), F32),
            pltpu.VMEM((ny, 1, 128), F32),
            pltpu.VMEM((ny, 1, 128), F32),
            pltpu.VMEM((ns, ny, half_n, 128), BF16),
            pltpu.VMEM((ns, ny, half_n, 128), BF16),
            pltpu.VMEM((ny, ns, half_n, 128), BF16),
            pltpu.VMEM((rows, owned), F32),
            pltpu.VMEM((2 * nx, il_n, owned), F32),
            pltpu.VMEM((il_n, owned), F32),
            pltpu.VMEM((nx, 2, il_n, owned), F32),
            pltpu.VMEM((nx, il_n, owned), F32),
            pltpu.VMEM((8, 128), F32),
            pltpu.VMEM((ns, 8, 128), F32),
            pltpu.VMEM((8, 128), F32),
            pltpu.VMEM((ny, 8, 128), F32),
            pltpu.VMEM((8, 128), F32),
            pltpu.VMEM((nx, 8, 128), F32),
            dma((5,)),
        ]
        for n in (nx, nx, ns, ns, ny, ny, nx, nx, ns, ny, nx):
            scratch += [dma((n,)), dma((n,))]
        dens, cum, mean, rem = pl.pallas_call(
            functools.partial(kernel, dims),
            out_shape=(
                jax.ShapeDtypeStruct((2, TYPES, owned), F32),
                jax.ShapeDtypeStruct((TYPES, owned), F32),
                jax.ShapeDtypeStruct((2, TYPES), F32),
                jax.ShapeDtypeStruct((1, TYPES), F32),
            ),
            in_specs=[any_, any_, any_, any_, sm],
            out_specs=(vm, vm, vm, vm),
            scratch_shapes=scratch,
            compiler_params=pltpu.CompilerParams(collective_id=0, has_side_effects=True),
        )(fractions, order.reshape(ny, 128), density, area, harvest)
        return dens, cum, mean, rem.reshape(TYPES)

    cell = ("z", "y", "core")
    return jax.shard_map(
        body,
        mesh=finer,
        in_specs=(P(None, cell), P(cell), P("pool", None, cell), P(None, cell), P("pool")),
        out_specs=(P("pool", None, cell), P(None, cell), P("pool", None), P()),
        check_vma=False,
    )
```

```python
import functools

import jax
import jax.numpy as jnp
from jax import lax
from jax.experimental import pallas as pl
from jax.experimental.pallas import tpu as pltpu
from jax.sharding import Mesh
from jax.sharding import PartitionSpec as P

MESH = pl.DeviceIdType.MESH
F32, BF16, I32 = jnp.float32, jnp.bfloat16, jnp.int32
TYPES = 16
VMEM_LIMIT = 12 * 1024 * 1024


def nt(a, b):
    return lax.dot_general(a, b, (((1,), (1,)), ((), ())), preferred_element_type=F32)


def iota(shape, dim):
    return lax.broadcasted_iota(I32, shape, dim)


def hand_over(*refs):
    sem = refs[8]
    copies = [pltpu.make_async_copy(refs[i], refs[4 + i], sem.at[i]) for i in range(4)]
    for cp in copies:
        cp.start()
    for cp in copies:
        cp.wait()


def kernel(dims, frac, order, dens, area, harv, out_dens, out_cum, out_mean, out_rem,
           f2, ordv, areav, hsm, hs, hg, dg, stock, oh, psend, pa, ps2, pb, sd, av, bv,
           mv, snd, snd_a, rcv, rcv_a, red0, red1, red2, red3, lsem,
           d_s, d_r, h_s, h_r, p1_s, p1_r, s1_s, s1_r, p2_s, p2_r, s2_s, s2_r,
           o_s, o_r, a_s, a_r, r1_s, r1_r, r2_s, r2_r):
    nz, ny, nc, nx, cells = dims
    ns = nz * nc
    rank_n = 128 // ns
    half_n = rank_n // 2
    owned = 128 * ny
    rows = 256 // nx
    il_n = TYPES // nx
    pools = 2 * nx
    z, y, c, x = (lax.axis_index(a) for a in ("z", "y", "core", "pool"))
    me = z * nc + c

    def dev_s(o):
        t = lax.rem(me + o, ns)
        return t, (t // nc, y, lax.rem(t, nc), x)

    def dev_y(o):
        t = lax.rem(y + o, ny)
        return t, (z, t, c, x)

    def dev_x(o):
        t = lax.rem(x + o, nx)
        return t, (z, y, c, t)

    def dev_yx(o):
        return z, lax.rem(y + o // nx, ny), c, lax.rem(x + o % nx, nx)

    local = [
        pltpu.make_async_copy(order, ordv, lsem.at[0]),
        pltpu.make_async_copy(frac.at[pl.ds(pl.multiple_of(x * rows, rows), rows), :], f2.at[pl.ds(0, rows), :], lsem.at[1]),
        pltpu.make_async_copy(frac.at[pl.ds(pl.multiple_of(x * rows, rows), rows), :], f2.at[pl.ds(rows, rows), :], lsem.at[2]),
        pltpu.make_async_copy(area, areav, lsem.at[3]),
        pltpu.make_async_copy(dens, dg.at[pl.ds(2 * x, 2)], lsem.at[4]),
        pltpu.make_async_copy(harv, hsm, lsem.at[5]),
    ]
    for cp in local:
        cp.start()

    barrier = pltpu.get_barrier_semaphore()
    peers = [dev_yx(o) for o in range(1, ny * nx)]
    peers += [dev_s(o)[1] for o in range(1, ns)]
    for p in peers:
        pl.semaphore_signal(barrier, inc=1, device_id=p, device_id_type=MESH)

    local[0].wait()
    ordr = ordv[...]
    dest = ordr // owned
    pos = lax.rem(ordr, owned)
    dz, dy, dc = dest // (ny * nc), lax.rem(dest // nc, ny), lax.rem(dest, nc)
    group = (dz * nc + dc) * ny + dy
    groups = ns * ny
    upper = (iota((128, 128), 0) < iota((128, 128), 1)).astype(BF16)
    ones = jnp.ones((128, 128), BF16)
    before = jnp.zeros((groups, 128), F32)
    ranks = []
    for b in range(ny):
        hot = iota((groups, 128), 0) == group[b:b + 1, :]
        hotb = hot.astype(BF16)
        oh[:, b * 128:(b + 1) * 128] = hotb
        count = jnp.dot(hotb, upper, preferred_element_type=F32) + before
        if b < ny - 1:
            before = before + jnp.dot(hotb, ones, preferred_element_type=F32)
        ranks.append(jnp.sum(jnp.where(hot, count, 0.0), axis=0, keepdims=True))
    rank = jnp.concatenate(ranks, axis=0).astype(I32)
    part = rank // half_n
    sub = lax.rem(rank, half_n)

    lane_of = part * (ns * half_n) + me * half_n + sub
    hi = (pos // 32).astype(F32)
    lo = lax.rem(pos, 32).astype(F32)
    acc_hi = jnp.zeros((groups, 128), F32)
    acc_lo = jnp.zeros((groups, 128), F32)
    for b in range(ny):
        hot = oh[:, b * 128:(b + 1) * 128]
        sel = iota((128, 128), 0) == lane_of[b:b + 1, :]
        acc_hi += nt(hot, jnp.where(sel, hi[b:b + 1, :], 0.0).astype(BF16))
        acc_lo += nt(hot, jnp.where(sel, lo[b:b + 1, :], 0.0).astype(BF16))
    psend[...] = (acc_hi * 32.0 + acc_lo).reshape(ns, ny, 128)

    sends = []

    def send(src, dst, ss, rs, to):
        cp = pltpu.make_async_remote_copy(src_ref=src, dst_ref=dst, send_sem=ss, recv_sem=rs,
                                          device_id=to, device_id_type=MESH)
        cp.start()
        sends.append(cp)
        return cp

    far_s = sorted(range(1, ns), key=lambda o: -min(o, ns - o))
    far_y = sorted(range(1, ny), key=lambda o: -min(o, ny - o))
    far_yx = sorted(range(1, ny * nx), key=lambda o: -min(o // nx, ny - o // nx) - min(o % nx, nx - o % nx))
    slot = {o: ny - 1 - far_y.index(o) for o in far_y}
    far_x = sorted(range(1, nx), key=lambda o: -min(o, nx - o))

    key = group * half_n + sub
    rho = groups * half_n
    local[1].wait()
    local[2].wait()
    halves = []
    for h in range(2):
        keyh = jnp.where(part == h, key, -1)
        hots = [(iota((rho, 128), 0) == keyh[b:b + 1, :]).astype(BF16) for b in range(ny)]
        halves.append(nt(jnp.concatenate(hots, axis=1), f2[...]))
    lanes = iota((rho, 128), 1)
    moved_cols = jnp.where(lanes < rows, halves[0], halves[1]).astype(BF16)
    sd[...] = moved_cols.reshape(ns, ny, half_n, 128)

    local[5].wait()
    row8, lane8 = iota((8, 128), 0), iota((8, 128), 1)
    hs[...] = jnp.where(row8 == 2 * x, hsm[0], jnp.where(row8 == 2 * x + 1, hsm[1], 0.0))

    pl.semaphore_wait(barrier, len(peers))
    p1, s1 = [], []
    for o in far_s:
        t, to = dev_s(o)
        p1.append(send(psend.at[t], pa.at[me], p1_s.at[o], p1_r.at[o], to))
        s1.append(send(sd.at[t], av.at[me], s1_s.at[o], s1_r.at[o], to))
    dcp, hcp = [], []
    for o in far_x:
        t, to = dev_x(o)
        hcp.append(send(hs, hg.at[x], h_s.at[o], h_r.at[o], to))
        dcp.append(send(dens, dg.at[pl.ds(2 * x, 2)], d_s.at[o], d_r.at[o], to))
    av[pl.ds(me, 1)] = sd[pl.ds(me, 1)]
    pa[pl.ds(me, 1)] = psend[pl.ds(me, 1)]
    hg[pl.ds(x, 1)] = hs[...].reshape(1, 8, 128)

    for cp in p1:
        cp.wait_recv()
    ptot = pa[0]
    for s in range(1, ns):
        ptot = ptot + pa[s]
    ps2[...] = ptot.reshape(ny, 1, 128)
    p2 = []
    for o in far_y:
        t, to = dev_y(o)
        p2.append(send(ps2.at[t], pb.at[slot[o]], p2_s.at[o], p2_r.at[o], to))
    pb[0:1] = ps2[pl.ds(y, 1)]

    for cp in s1:
        cp.wait_recv()
    s2 = []
    for o in far_y:
        t, to = dev_y(o)
        s2.append(send(av.at[:, t], bv.at[slot[o]], s2_s.at[o], s2_r.at[o], to))
    bv[0:1] = av[:, pl.ds(y, 1)].reshape(1, ns, half_n, 128)

    for cp in hcp:
        cp.wait_recv()
    harvest = hg[0]
    for s in range(1, nx):
        harvest = harvest + hg[s]
    local[3].wait()
    local[4].wait()
    for cp in dcp:
        cp.wait_recv()
    for j in range(TYPES):
        stock[j] = dg[:, j, :] * areav[j:j + 1, :]

    for cp in p2:
        cp.wait_recv()
    low = iota((1, 128), 1) < 64
    hots = [[], []]
    for q in range(ny // 2):
        a, b = pb[2 * q], pb[2 * q + 1]
        ra, rb = pltpu.roll(a, 64, 1), pltpu.roll(b, 64, 1)
        for h, v in enumerate((jnp.where(low, a, rb), jnp.where(low, ra, b))):
            hots[h].append((iota((owned, 128), 0) == v.astype(I32)).astype(BF16))
    spread = [jnp.concatenate(v, axis=1) for v in hots]

    per = ny // 2
    width = per * ns * half_n
    for g in range(2):
        for o, cp in zip(far_y, s2):
            if slot[o] // per == g:
                cp.wait_recv()
        turned = bv[g * per:(g + 1) * per].reshape(width, 128).T
        got = [nt(turned[h * rows:(h + 1) * rows], spread[h][:, g * width:(g + 1) * width]) for h in range(2)]
        if g == 0:
            near = got[0] + got[1]
    mv[...] = near + (got[0] + got[1])

    keep = 1.0 - harvest
    zero = jnp.zeros((8, 128), F32)

    def block(lb, carry):
        sums, gone = carry
        cols = pl.ds(pl.multiple_of(lb * 128, 128), 128)
        new_sums, new_gone = [], []
        for il in range(il_n):
            tot, na, stay = zero, zero, zero
            for j in range(TYPES):
                m = jnp.broadcast_to(mv[il * TYPES + j:il * TYPES + j + 1, cols], (8, 128))
                term = m * stock[j, :, cols]
                tot = tot + term
                if j % il_n == il:
                    stay = jnp.where(x == j // il_n, term, stay)
                na = na + m * jnp.broadcast_to(areav[j:j + 1, cols], (8, 128))
            moved = tot - stay
            ns_i = stay + keep * moved
            new_sums.append(sums[il] + ns_i)
            new_gone.append(gone[il] + harvest * moved)
            snd[:, il, cols] = ns_i / na
            snd_a[il:il + 1, cols] = na[0:1]
        return tuple(new_sums), tuple(new_gone)

    zeros = (zero,) * il_n
    sums, gone = lax.fori_loop(0, ny, block, (zeros, zeros))

    ocp = []
    for o in far_x:
        t, to = dev_x(o)
        ocp.append(send(snd_a, rcv_a.at[x], a_s.at[o], a_r.at[o], to))
        ocp.append(send(snd.at[pl.ds(2 * t, 2)], rcv.at[x], o_s.at[o], o_r.at[o], to))

    word = zero
    for il in range(il_n):
        word = jnp.where(lane8 == row8 * il_n + il, jnp.sum(sums[il], axis=1, keepdims=True), word)
        word = jnp.where(lane8 == 8 * il_n + il, jnp.sum(gone[il], axis=1, keepdims=True), word)
    word = jnp.sum(word, axis=0, keepdims=True)
    red0[...] = word
    rc = []
    for o in far_s:
        t, to = dev_s(o)
        rc.append(send(red0, red1.at[me], r1_s.at[o], r1_r.at[o], to))
    red1[pl.ds(me, 1)] = word.reshape(1, 1, 128)
    rcv[pl.ds(x, 1)] = snd[pl.ds(2 * x, 2)].reshape(1, 2, il_n, owned)
    rcv_a[pl.ds(x, 1)] = snd_a[...].reshape(1, il_n, owned)
    for cp in rc:
        cp.wait_recv()
    tot = red1[0]
    for s in range(1, ns):
        tot = tot + red1[s]
    red2[...] = tot
    rc = []
    for o in far_yx:
        to = dev_yx(o)
        rc.append(send(red2, red3.at[y * nx + x], r2_s.at[o], r2_r.at[o], to))
    red3[pl.ds(y * nx + x, 1)] = tot.reshape(1, 1, 128)

    for cp in ocp:
        cp.wait_recv()
    run = None
    for i in range(TYPES):
        xs, il = i // il_n, i % il_n
        r = rcv_a[xs, il:il + 1, :]
        run = r if run is None else run + r
        out_cum[i:i + 1, :] = run
        for q in range(2):
            out_dens[q, i:i + 1, :] = rcv[xs, q, il:il + 1, :]
    out_cum[...] = out_cum[...] / run

    for cp in rc:
        cp.wait_recv()
    lane1 = iota((1, 128), 1)
    mean = [jnp.zeros((1, 128), F32)] * 2
    rem = jnp.zeros((1, 128), F32)
    for xs in range(nx):
        tot = red3[xs]
        for s in range(1, ny):
            tot = tot + red3[s * nx + xs]
        tot = tot / cells
        here = lane1 // il_n == xs
        rem = jnp.where(here, pltpu.roll(tot, 128 - 8 * il_n + xs * il_n, 1), rem)
        for q in range(2):
            away = lax.rem(128 + (xs - q) * il_n - 2 * il_n * x, 128)
            mean[q] = jnp.where(here, pltpu.roll(tot, away, 1), mean[q])
    out_rem[...] = rem[:, :TYPES]
    for q in range(2):
        out_mean[q:q + 1, :] = mean[q][:, :TYPES]
    for cp in sends:
        cp.wait_send()


def solution(mesh):
    nx = mesh.shape["pool"]
    nc = 2
    ncell = mesh.shape["cell"]
    nz = ny = int(round((ncell // nc) ** 0.5))
    finer = Mesh(mesh.devices.reshape(nz, ny, nc, nx), ("z", "y", "core", "pool"))
    ns = nz * nc
    half_n = 64 // ns
    owned = 128 * ny
    rows = 256 // nx
    il_n = TYPES // nx
    groups = ns * ny
    dims = (nz, ny, nc, nx, float(ncell * owned))
    any_, vm = pl.BlockSpec(memory_space=pl.ANY), pl.BlockSpec(memory_space=pltpu.VMEM)
    hbm = pl.BlockSpec(memory_space=pltpu.HBM)
    dma = pltpu.SemaphoreType.DMA

    def body(fractions, order, density, area, harvest):
        scratch = [
            pltpu.VMEM((2 * rows, owned), BF16),
            pltpu.VMEM((ny, 128), I32),
            pltpu.VMEM((TYPES, owned), F32),
            pltpu.SMEM((2,), F32),
            pltpu.VMEM((8, 128), F32),
            pltpu.VMEM((nx, 8, 128), F32),
            pltpu.VMEM((2 * nx, TYPES, owned), F32),
            pltpu.VMEM((TYPES, 2 * nx, owned), F32),
            pltpu.VMEM((groups, owned), BF16),
            pltpu.VMEM((ns, ny, 128), F32),
            pltpu.VMEM((ns, ny, 128), F32),
            pltpu.VMEM((ny, 1, 128), F32),
            pltpu.VMEM((ny, 1, 128), F32),
            pltpu.VMEM((ns, ny, half_n, 128), BF16),
            pltpu.VMEM((ns, ny, half_n, 128), BF16),
            pltpu.VMEM((ny, ns, half_n, 128), BF16),
            pltpu.VMEM((rows, owned), F32),
            pltpu.VMEM((2 * nx, il_n, owned), F32),
            pltpu.VMEM((il_n, owned), F32),
            pltpu.VMEM((nx, 2, il_n, owned), F32),
            pltpu.VMEM((nx, il_n, owned), F32),
            pltpu.VMEM((1, 128), F32),
            pltpu.VMEM((ns, 1, 128), F32),
            pltpu.VMEM((1, 128), F32),
            pltpu.VMEM((ny * nx, 1, 128), F32),
            dma((6,)),
        ]
        for n in (nx, nx, ns, ns, ny, ny, nx, nx, ns, ny * nx):
            scratch += [dma((n,)), dma((n,))]
        results = pl.pallas_call(
            functools.partial(kernel, dims),
            out_shape=(
                jax.ShapeDtypeStruct((2, TYPES, owned), F32),
                jax.ShapeDtypeStruct((TYPES, owned), F32),
                jax.ShapeDtypeStruct((2, TYPES), F32),
                jax.ShapeDtypeStruct((1, TYPES), F32),
            ),
            in_specs=[hbm] * 5,
            out_specs=(vm, vm, vm, vm),
            scratch_shapes=scratch,
            compiler_params=pltpu.CompilerParams(collective_id=0, has_side_effects=True, vmem_limit_bytes=VMEM_LIMIT),
        )(*(pltpu.with_memory_space_constraint(a, pltpu.HBM) for a in (fractions, order.reshape(ny, 128), density, area, harvest)))
        dens, cum, mean, rem = pl.pallas_call(
            hand_over,
            out_shape=tuple(jax.ShapeDtypeStruct(r.shape, r.dtype) for r in results),
            in_specs=[any_] * 4,
            out_specs=(hbm,) * 4,
            scratch_shapes=[dma((4,))],
            compiler_params=pltpu.CompilerParams(vmem_limit_bytes=VMEM_LIMIT),
        )(*results)
        return dens, cum, mean, rem.reshape(TYPES)

    cell = ("z", "y", "core")
    return jax.shard_map(
        body,
        mesh=finer,
        in_specs=(P(None, cell), P(cell), P("pool", None, cell), P(None, cell), P("pool")),
        out_specs=(P("pool", None, cell), P(None, cell), P("pool", None), P()),
        check_vma=False,
    )
```

```python
import functools

import jax
import jax.numpy as jnp
from jax import lax
from jax.experimental import pallas as pl
from jax.experimental.pallas import tpu as pltpu
from jax.sharding import Mesh
from jax.sharding import PartitionSpec as P

MESH = pl.DeviceIdType.MESH
F32, BF16, I32 = jnp.float32, jnp.bfloat16, jnp.int32
TYPES = 16
VMEM_LIMIT = 12 * 1024 * 1024


def nt(a, b):
    return lax.dot_general(a, b, (((1,), (1,)), ((), ())), preferred_element_type=F32)


def iota(shape, dim):
    return lax.broadcasted_iota(I32, shape, dim)


def hand_over(*refs):
    sem = refs[8]
    copies = [pltpu.make_async_copy(refs[i], refs[4 + i], sem.at[i]) for i in range(4)]
    for cp in copies:
        cp.start()
    for cp in copies:
        cp.wait()


def kernel(dims, frac, order, dens, area, harv, out_dens, out_cum, out_mean, out_rem,
           f2, ordv, areav, hsm, hs, hg, dg, stock, sd, av, bv,
           mv, snd, snd_a, rcv, rcv_a, red0, red1, red2, red3, lsem,
           d_s, d_r, h_s, h_r, s1_s, s1_r, s2_s, s2_r,
           o_s, o_r, a_s, a_r, r1_s, r1_r, r2_s, r2_r):
    nz, ny, nc, nx, cells = dims
    ns = nz * nc
    rank_n = 128 // ns
    half_n = rank_n // 2
    owned = 128 * ny
    rows = 256 // nx
    il_n = TYPES // nx
    pools = 2 * nx
    z, y, c, x = (lax.axis_index(a) for a in ("z", "y", "core", "pool"))
    me = z * nc + c

    def dev_s(o):
        t = lax.rem(me + o, ns)
        return t, (t // nc, y, lax.rem(t, nc), x)

    def dev_y(o):
        t = lax.rem(y + o, ny)
        return t, (z, t, c, x)

    def dev_x(o):
        t = lax.rem(x + o, nx)
        return t, (z, y, c, t)

    def dev_yx(o):
        return z, lax.rem(y + o // nx, ny), c, lax.rem(x + o % nx, nx)

    local = [
        pltpu.make_async_copy(order, ordv, lsem.at[0]),
        pltpu.make_async_copy(frac.at[pl.ds(pl.multiple_of(x * rows, rows), rows), :], f2.at[pl.ds(0, rows), :], lsem.at[1]),
        pltpu.make_async_copy(frac.at[pl.ds(pl.multiple_of(x * rows, rows), rows), :], f2.at[pl.ds(rows, rows), :], lsem.at[2]),
        pltpu.make_async_copy(area, areav, lsem.at[3]),
        pltpu.make_async_copy(dens, dg.at[pl.ds(2 * x, 2)], lsem.at[4]),
        pltpu.make_async_copy(harv, hsm, lsem.at[5]),
    ]
    for cp in local:
        cp.start()

    barrier = pltpu.get_barrier_semaphore()
    peers = [dev_x(o)[1] for o in range(1, nx)]
    peers += [dev_y(o)[1] for o in range(1, ny)]
    peers += [dev_s(o)[1] for o in range(1, ns)]
    for p in peers:
        pl.semaphore_signal(barrier, inc=1, device_id=p, device_id_type=MESH)

    local[0].wait()
    ordr = ordv[...]
    dest = ordr // owned
    pos = lax.rem(ordr, owned)
    dz, dy, dc = dest // (ny * nc), lax.rem(dest // nc, ny), lax.rem(dest, nc)
    group = (dz * nc + dc) * ny + dy
    groups = ns * ny
    upper = (iota((128, 128), 0) < iota((128, 128), 1)).astype(BF16)
    ones = jnp.ones((128, 128), BF16)
    before = jnp.zeros((groups, 128), F32)
    ranks = []
    for b in range(ny):
        hot = iota((groups, 128), 0) == group[b:b + 1, :]
        hotb = hot.astype(BF16)
        count = jnp.dot(hotb, upper, preferred_element_type=F32) + before
        if b < ny - 1:
            before = before + jnp.dot(hotb, ones, preferred_element_type=F32)
        ranks.append(jnp.sum(jnp.where(hot, count, 0.0), axis=0, keepdims=True))
    rank = jnp.concatenate(ranks, axis=0).astype(I32)
    part = rank // half_n
    sub = lax.rem(rank, half_n)

    home = dz * nc + dc
    lane_of = part * 64 + lax.rem(me + dy, ns) * half_n + sub
    hi = (pos // 32).astype(F32)
    lo = lax.rem(pos, 32).astype(F32)
    digit = lax.rem(iota((ns * half_n, 128), 0), half_n)
    owner = iota((ns * half_n, 128), 0) // half_n
    left, right = [], []
    for b in range(ny):
        r = slice(b, b + 1)
        value = jnp.where(digit == 0, hi[r], jnp.where(digit == 1, lo[r], 0.0))
        left.append(jnp.where(owner == home[r], value, 0.0).astype(BF16))
        right.append((iota((128, 128), 0) == lane_of[r]).astype(BF16))
    placed = nt(jnp.concatenate(left, axis=1), jnp.concatenate(right, axis=1))
    sd[:, ny] = placed.astype(BF16).reshape(ns, half_n, 128)

    sends = []

    def send(src, dst, ss, rs, to):
        cp = pltpu.make_async_remote_copy(src_ref=src, dst_ref=dst, send_sem=ss, recv_sem=rs,
                                          device_id=to, device_id_type=MESH)
        cp.start()
        sends.append(cp)
        return cp

    far_s = sorted(range(1, ns), key=lambda o: -min(o, ns - o))
    far_y = sorted(range(1, ny), key=lambda o: -min(o, ny - o))
    far_yx = sorted(range(1, ny * nx), key=lambda o: -min(o // nx, ny - o // nx) - min(o % nx, nx - o % nx))
    slot = {o: ny - 1 - far_y.index(o) for o in far_y}
    far_x = sorted(range(1, nx), key=lambda o: -min(o, nx - o))

    key = group * half_n + sub
    rho = groups * half_n
    local[1].wait()
    local[2].wait()
    halves = []
    for h in range(2):
        keyh = jnp.where(part == h, key, -1)
        hots = [(iota((rho, 128), 0) == keyh[b:b + 1, :]).astype(BF16) for b in range(ny)]
        halves.append(nt(jnp.concatenate(hots, axis=1), f2[...]))
    lanes = iota((rho, 128), 1)
    moved_cols = jnp.where(lanes < rows, halves[0], halves[1]).astype(BF16)
    sd[:, :ny] = moved_cols.reshape(ns, ny, half_n, 128)

    local[5].wait()
    row8, lane8 = iota((8, 128), 0), iota((8, 128), 1)
    hs[...] = jnp.where(row8 == 2 * x, hsm[0], jnp.where(row8 == 2 * x + 1, hsm[1], 0.0))

    pl.semaphore_wait(barrier, len(peers))
    s1 = []
    for o in far_s:
        t, to = dev_s(o)
        s1.append(send(sd.at[t], av.at[me], s1_s.at[o], s1_r.at[o], to))
    dcp, hcp = [], []
    for o in far_x:
        t, to = dev_x(o)
        hcp.append(send(hs, hg.at[x], h_s.at[o], h_r.at[o], to))
        dcp.append(send(dens, dg.at[pl.ds(2 * x, 2)], d_s.at[o], d_r.at[o], to))
    av[pl.ds(me, 1)] = sd[pl.ds(me, 1)]
    hg[pl.ds(x, 1)] = hs[...].reshape(1, 8, 128)

    shape3 = (ny, half_n, 128)
    source = lax.rem(lax.rem(iota(shape3, 2), 64) // half_n + ns - iota(shape3, 0), ns)
    placed = jnp.zeros(shape3, F32)
    for o in [0] + far_s[::-1]:
        src = lax.rem(me + ns - o, ns)
        if o:
            s1[far_s.index(o)].wait_recv()
        placed = jnp.where(source == src, av[pl.ds(src, 1), ny].astype(F32), placed)
    av[ns, :ny] = placed.astype(BF16)
    s2 = []
    for o in far_y:
        t, to = dev_y(o)
        s2.append(send(av.at[:, t], bv.at[slot[o]], s2_s.at[o], s2_r.at[o], to))
    bv[0:1] = av[:, pl.ds(y, 1)].reshape(1, ns + 1, half_n, 128)

    for cp in hcp:
        cp.wait_recv()
    harvest = hg[0]
    for s in range(1, nx):
        harvest = harvest + hg[s]
    local[3].wait()
    local[4].wait()
    for cp in dcp:
        cp.wait_recv()
    for j in range(TYPES):
        stock[j] = dg[:, j, :] * areav[j:j + 1, :]

    low = iota((1, 128), 1) < 64
    same = lax.rem(iota((1, 128), 1), 64) < 64 - half_n * y
    for q in range(ny // 2):
        rolled = []
        for k in (2 * q, 2 * q + 1):
            for o, cp in zip(far_y, s2):
                if slot[o] == k:
                    cp.wait_recv()
            digits = bv[k, ns].astype(F32)
            p = digits[0:1] * 32.0 + digits[1:2]
            rolled.append((pltpu.roll(p, 128 - half_n * y, 1), pltpu.roll(p, 64 - half_n * y, 1)))
        (a1, a2), (b1, b2) = rolled
        firsts = jnp.where(low, jnp.where(same, a1, a2), jnp.where(same, b2, b1)).astype(I32)
        seconds = jnp.where(low, jnp.where(same, a2, a1), jnp.where(same, b1, b2)).astype(I32)
        spread = jnp.concatenate([(iota((owned, 128), 0) == v).astype(BF16) for v in (firsts, seconds)], axis=1)
        turned = bv[2 * q:2 * q + 2, :ns].reshape(128, 128).T
        got = nt(jnp.concatenate([turned[:rows], turned[rows:]], axis=1), spread)
        mv[...] = got if q == 0 else mv[...] + got

    keep = 1.0 - harvest
    zero = jnp.zeros((8, 128), F32)

    def block(lb, carry):
        sums, gone = carry
        cols = pl.ds(pl.multiple_of(lb * 128, 128), 128)
        new_sums, new_gone = [], []
        for il in range(il_n):
            tot, na, stay = zero, zero, zero
            for j in range(TYPES):
                m = jnp.broadcast_to(mv[il * TYPES + j:il * TYPES + j + 1, cols], (8, 128))
                term = m * stock[j, :, cols]
                tot = tot + term
                if j % il_n == il:
                    stay = jnp.where(x == j // il_n, term, stay)
                na = na + m * jnp.broadcast_to(areav[j:j + 1, cols], (8, 128))
            moved = tot - stay
            ns_i = stay + keep * moved
            new_sums.append(sums[il] + ns_i)
            new_gone.append(gone[il] + harvest * moved)
            snd[:, il, cols] = ns_i / na
            snd_a[il:il + 1, cols] = na[0:1]
        return tuple(new_sums), tuple(new_gone)

    zeros = (zero,) * il_n
    sums, gone = lax.fori_loop(0, ny, block, (zeros, zeros))

    word = zero
    for il in range(il_n):
        word = jnp.where(lane8 == row8 * il_n + il, jnp.sum(sums[il], axis=1, keepdims=True), word)
        word = jnp.where(lane8 == 8 * il_n + il, jnp.sum(gone[il], axis=1, keepdims=True), word)
    word = jnp.sum(word, axis=0, keepdims=True)
    red0[...] = word
    rc = []
    for o in far_s:
        t, to = dev_s(o)
        rc.append(send(red0, red1.at[me], r1_s.at[o], r1_r.at[o], to))
    red1[pl.ds(me, 1)] = word.reshape(1, 1, 128)
    ocp = []
    for o in far_x:
        t, to = dev_x(o)
        ocp.append(send(snd_a, rcv_a.at[x], a_s.at[o], a_r.at[o], to))
        ocp.append(send(snd.at[pl.ds(2 * t, 2)], rcv.at[x], o_s.at[o], o_r.at[o], to))

    rcv[pl.ds(x, 1)] = snd[pl.ds(2 * x, 2)].reshape(1, 2, il_n, owned)
    rcv_a[pl.ds(x, 1)] = snd_a[...].reshape(1, il_n, owned)
    for cp in rc:
        cp.wait_recv()
    tot = red1[0]
    for s in range(1, ns):
        tot = tot + red1[s]
    red2[...] = tot
    rc = []
    for o in far_yx:
        to = dev_yx(o)
        rc.append(send(red2, red3.at[y * nx + x], r2_s.at[o], r2_r.at[o], to))
    red3[pl.ds(y * nx + x, 1)] = tot.reshape(1, 1, 128)

    for cp in ocp:
        cp.wait_recv()
    run = None
    for i in range(TYPES):
        xs, il = i // il_n, i % il_n
        r = rcv_a[xs, il:il + 1, :]
        run = r if run is None else run + r
        out_cum[i:i + 1, :] = run
        for q in range(2):
            out_dens[q, i:i + 1, :] = rcv[xs, q, il:il + 1, :]
    out_cum[...] = out_cum[...] / run

    for cp in rc:
        cp.wait_recv()
    lane1 = iota((1, 128), 1)
    mean = [jnp.zeros((1, 128), F32)] * 2
    rem = jnp.zeros((1, 128), F32)
    for xs in range(nx):
        tot = red3[xs]
        for s in range(1, ny):
            tot = tot + red3[s * nx + xs]
        tot = tot / cells
        here = lane1 // il_n == xs
        rem = jnp.where(here, pltpu.roll(tot, 128 - 8 * il_n + xs * il_n, 1), rem)
        for q in range(2):
            away = lax.rem(128 + (xs - q) * il_n - 2 * il_n * x, 128)
            mean[q] = jnp.where(here, pltpu.roll(tot, away, 1), mean[q])
    out_rem[...] = rem[:, :TYPES]
    for q in range(2):
        out_mean[q:q + 1, :] = mean[q][:, :TYPES]
    for cp in sends:
        cp.wait_send()


def solution(mesh):
    nx = mesh.shape["pool"]
    nc = 2
    ncell = mesh.shape["cell"]
    nz = ny = int(round((ncell // nc) ** 0.5))
    finer = Mesh(mesh.devices.reshape(nz, ny, nc, nx), ("z", "y", "core", "pool"))
    ns = nz * nc
    half_n = 64 // ns
    owned = 128 * ny
    rows = 256 // nx
    il_n = TYPES // nx
    groups = ns * ny
    dims = (nz, ny, nc, nx, float(ncell * owned))
    any_, vm = pl.BlockSpec(memory_space=pl.ANY), pl.BlockSpec(memory_space=pltpu.VMEM)
    hbm = pl.BlockSpec(memory_space=pltpu.HBM)
    dma = pltpu.SemaphoreType.DMA

    def body(fractions, order, density, area, harvest):
        scratch = [
            pltpu.VMEM((2 * rows, owned), BF16),
            pltpu.VMEM((ny, 128), I32),
            pltpu.VMEM((TYPES, owned), F32),
            pltpu.SMEM((2,), F32),
            pltpu.VMEM((8, 128), F32),
            pltpu.VMEM((nx, 8, 128), F32),
            pltpu.VMEM((2 * nx, TYPES, owned), F32),
            pltpu.VMEM((TYPES, 2 * nx, owned), F32),
            pltpu.VMEM((ns, ny + 1, half_n, 128), BF16),
            pltpu.VMEM((ns + 1, ny + 1, half_n, 128), BF16),
            pltpu.VMEM((ny, ns + 1, half_n, 128), BF16),
            pltpu.VMEM((rows, owned), F32),
            pltpu.VMEM((2 * nx, il_n, owned), F32),
            pltpu.VMEM((il_n, owned), F32),
            pltpu.VMEM((nx, 2, il_n, owned), F32),
            pltpu.VMEM((nx, il_n, owned), F32),
            pltpu.VMEM((1, 128), F32),
            pltpu.VMEM((ns, 1, 128), F32),
            pltpu.VMEM((1, 128), F32),
            pltpu.VMEM((ny * nx, 1, 128), F32),
            dma((6,)),
        ]
        for n in (nx, nx, ns, ny, nx, nx, ns, ny * nx):
            scratch += [dma((n,)), dma((n,))]
        results = pl.pallas_call(
            functools.partial(kernel, dims),
            out_shape=(
                jax.ShapeDtypeStruct((2, TYPES, owned), F32),
                jax.ShapeDtypeStruct((TYPES, owned), F32),
                jax.ShapeDtypeStruct((2, TYPES), F32),
                jax.ShapeDtypeStruct((1, TYPES), F32),
            ),
            in_specs=[hbm] * 5,
            out_specs=(vm, vm, vm, vm),
            scratch_shapes=scratch,
            compiler_params=pltpu.CompilerParams(collective_id=0, has_side_effects=True, vmem_limit_bytes=VMEM_LIMIT),
        )(*(pltpu.with_memory_space_constraint(a, pltpu.HBM) for a in (fractions, order.reshape(ny, 128), density, area, harvest)))
        dens, cum, mean, rem = pl.pallas_call(
            hand_over,
            out_shape=tuple(jax.ShapeDtypeStruct(r.shape, r.dtype) for r in results),
            in_specs=[any_] * 4,
            out_specs=(hbm,) * 4,
            scratch_shapes=[dma((4,))],
            compiler_params=pltpu.CompilerParams(vmem_limit_bytes=VMEM_LIMIT),
        )(*results)
        return dens, cum, mean, rem.reshape(TYPES)

    cell = ("z", "y", "core")
    return jax.shard_map(
        body,
        mesh=finer,
        in_specs=(P(None, cell), P(cell), P("pool", None, cell), P(None, cell), P("pool")),
        out_specs=(P("pool", None, cell), P(None, cell), P("pool", None), P()),
        check_vma=False,
    )
```

```python
import functools

import jax
import jax.numpy as jnp
from jax import lax
from jax.experimental import pallas as pl
from jax.experimental.pallas import tpu as pltpu
from jax.sharding import Mesh
from jax.sharding import PartitionSpec as P

MESH = pl.DeviceIdType.MESH
F32, BF16, I32 = jnp.float32, jnp.bfloat16, jnp.int32
TYPES = 16
VMEM_LIMIT = 12 * 1024 * 1024


def nt(a, b):
    return lax.dot_general(a, b, (((1,), (1,)), ((), ())), preferred_element_type=F32)


def iota(shape, dim):
    return lax.broadcasted_iota(I32, shape, dim)


def hand_over(*refs):
    sem = refs[8]
    copies = [pltpu.make_async_copy(refs[i], refs[4 + i], sem.at[i]) for i in range(4)]
    for cp in copies:
        cp.start()
    for cp in copies:
        cp.wait()


def kernel(dims, frac, order, dens, area, harv, out_dens, out_cum, out_mean, out_rem,
           f2, ordv, areav, hsm, hs, hg, dg, stock, sd, av, bv,
           mv, snd, snd_a, rcv, rcv_a, red0, red1, red2, red3, lsem,
           d_s, d_r, h_s, h_r, s1_s, s1_r, s2_s, s2_r,
           o_s, o_r, a_s, a_r, r1_s, r1_r, r2_s, r2_r):
    nz, ny, nc, nx, cells = dims
    ns = nz * nc
    rank_n = 128 // ns
    half_n = rank_n // 2
    owned = 128 * ny
    rows = 256 // nx
    il_n = TYPES // nx
    pools = 2 * nx
    z, y, c, x = (lax.axis_index(a) for a in ("z", "y", "core", "pool"))
    me = z * nc + c

    def dev_s(o):
        t = lax.rem(me + o, ns)
        return t, (t // nc, y, lax.rem(t, nc), x)

    def dev_y(o):
        t = lax.rem(y + o, ny)
        return t, (z, t, c, x)

    def dev_x(o):
        t = lax.rem(x + o, nx)
        return t, (z, y, c, t)

    def dev_yx(o):
        return z, lax.rem(y + o // nx, ny), c, lax.rem(x + o % nx, nx)

    local = [
        pltpu.make_async_copy(order, ordv, lsem.at[0]),
        pltpu.make_async_copy(frac.at[pl.ds(pl.multiple_of(x * rows, rows), rows), :], f2.at[pl.ds(0, rows), :], lsem.at[1]),
        pltpu.make_async_copy(frac.at[pl.ds(pl.multiple_of(x * rows, rows), rows), :], f2.at[pl.ds(rows, rows), :], lsem.at[2]),
        pltpu.make_async_copy(area, areav, lsem.at[3]),
        pltpu.make_async_copy(dens, dg.at[pl.ds(2 * x, 2)], lsem.at[4]),
        pltpu.make_async_copy(harv, hsm, lsem.at[5]),
    ]
    for cp in local:
        cp.start()

    barrier = pltpu.get_barrier_semaphore()
    peers = [dev_x(o)[1] for o in range(1, nx)]
    peers += [dev_y(o)[1] for o in range(1, ny)]
    peers += [dev_s(o)[1] for o in range(1, ns)]
    for p in peers:
        pl.semaphore_signal(barrier, inc=1, device_id=p, device_id_type=MESH)

    local[0].wait()
    ordr = ordv[...]
    dest = ordr // owned
    pos = lax.rem(ordr, owned)
    dz, dy, dc = dest // (ny * nc), lax.rem(dest // nc, ny), lax.rem(dest, nc)
    group = (dz * nc + dc) * ny + dy
    groups = ns * ny
    upper = (iota((128, 128), 0) < iota((128, 128), 1)).astype(BF16)
    ones = jnp.ones((128, 128), BF16)
    before = jnp.zeros((groups, 128), F32)
    ranks = []
    for b in range(ny):
        hot = iota((groups, 128), 0) == group[b:b + 1, :]
        hotb = hot.astype(BF16)
        count = jnp.dot(hotb, upper, preferred_element_type=F32) + before
        if b < ny - 1:
            before = before + jnp.dot(hotb, ones, preferred_element_type=F32)
        ranks.append(jnp.sum(jnp.where(hot, count, 0.0), axis=0, keepdims=True))
    rank = jnp.concatenate(ranks, axis=0).astype(I32)
    part = rank // half_n
    sub = lax.rem(rank, half_n)

    home = dz * nc + dc
    lane_of = part * 64 + lax.rem(me + dy, ns) * half_n + sub
    hi = (pos // 128).astype(F32)
    lo = lax.rem(pos, 128).astype(F32)
    digit = lax.rem(iota((ns * half_n, 128), 0), half_n)
    owner = iota((ns * half_n, 128), 0) // half_n
    left, right = [], []
    for b in range(ny):
        r = slice(b, b + 1)
        value = jnp.where(digit == 0, hi[r], jnp.where(digit == 1, lo[r], 0.0))
        left.append(jnp.where(owner == home[r], value, 0.0).astype(BF16))
        right.append((iota((128, 128), 0) == lane_of[r]).astype(BF16))
    placed = nt(jnp.concatenate(left, axis=1), jnp.concatenate(right, axis=1))
    sd[:, ny] = placed.astype(BF16).reshape(ns, half_n, 128)

    sends = []

    def send(src, dst, ss, rs, to):
        cp = pltpu.make_async_remote_copy(src_ref=src, dst_ref=dst, send_sem=ss, recv_sem=rs,
                                          device_id=to, device_id_type=MESH)
        cp.start()
        sends.append(cp)
        return cp

    far_s = sorted(range(1, ns), key=lambda o: -min(o, ns - o))
    far_y = sorted(range(1, ny), key=lambda o: -min(o, ny - o))
    far_yx = sorted(range(1, ny * nx), key=lambda o: -min(o // nx, ny - o // nx) - min(o % nx, nx - o % nx))
    slot = {o: ny - 1 - far_y.index(o) for o in far_y}
    far_x = sorted(range(1, nx), key=lambda o: -min(o, nx - o))

    key = group * half_n + sub
    rho = groups * half_n
    local[1].wait()
    local[2].wait()
    halves = []
    for h in range(2):
        keyh = jnp.where(part == h, key, -1)
        hots = [(iota((rho, 128), 0) == keyh[b:b + 1, :]).astype(BF16) for b in range(ny)]
        halves.append(nt(jnp.concatenate(hots, axis=1), f2[...]))
    lanes = iota((rho, 128), 1)
    moved_cols = jnp.where(lanes < rows, halves[0], halves[1]).astype(BF16)
    sd[:, :ny] = moved_cols.reshape(ns, ny, half_n, 128)

    local[5].wait()
    row8, lane8 = iota((8, 128), 0), iota((8, 128), 1)
    hs[...] = jnp.where(row8 == 2 * x, hsm[0], jnp.where(row8 == 2 * x + 1, hsm[1], 0.0))

    pl.semaphore_wait(barrier, len(peers))
    s1 = []
    for o in far_s:
        t, to = dev_s(o)
        s1.append(send(sd.at[t], av.at[:, me], s1_s.at[o], s1_r.at[o], to))
    dcp, hcp = [], []
    for o in far_x:
        t, to = dev_x(o)
        hcp.append(send(hs, hg.at[x], h_s.at[o], h_r.at[o], to))
        dcp.append(send(dens, dg.at[pl.ds(2 * x, 2)], d_s.at[o], d_r.at[o], to))
    av[:, pl.ds(me, 1)] = sd[pl.ds(me, 1)].reshape(ny + 1, 1, half_n, 128)
    hg[pl.ds(x, 1)] = hs[...].reshape(1, 8, 128)

    shape3 = (ny, half_n, 128)
    source = lax.rem(lax.rem(iota(shape3, 2), 64) // half_n + ns - iota(shape3, 0), ns)
    placed = jnp.zeros(shape3, F32)
    for o in [0] + far_s[::-1]:
        src = lax.rem(me + ns - o, ns)
        if o:
            s1[far_s.index(o)].wait_recv()
        placed = jnp.where(source == src, av[ny, pl.ds(src, 1)].astype(F32), placed)
    av[:ny, ns] = placed.astype(BF16)
    s2 = []
    for o in far_y:
        t, to = dev_y(o)
        s2.append(send(av.at[t], bv.at[slot[o]], s2_s.at[o], s2_r.at[o], to))
    bv[0:1] = av[pl.ds(y, 1)]

    for cp in hcp:
        cp.wait_recv()
    harvest = hg[0]
    for s in range(1, nx):
        harvest = harvest + hg[s]
    local[3].wait()
    local[4].wait()
    for cp in dcp:
        cp.wait_recv()
    for j in range(TYPES):
        stock[j] = dg[:, j, :] * areav[j:j + 1, :]

    low = iota((2, 128), 1) < 64
    same = lax.rem(iota((2, 128), 1), 64) < 64 - half_n * y
    for q in range(ny // 2):
        rolled = []
        for k in (2 * q, 2 * q + 1):
            for o, cp in zip(far_y, s2):
                if slot[o] == k:
                    cp.wait_recv()
            digits = bv[k, ns].astype(F32)[0:2]
            rolled.append((pltpu.roll(digits, 128 - half_n * y, 1), pltpu.roll(digits, 64 - half_n * y, 1)))
        (a1, a2), (b1, b2) = rolled
        firsts = jnp.where(low, jnp.where(same, a1, a2), jnp.where(same, b2, b1))
        seconds = jnp.where(low, jnp.where(same, a2, a1), jnp.where(same, b1, b2))
        place = jnp.concatenate([firsts, seconds], axis=1).astype(I32)
        spread = (iota((128, 256), 0) == place[1:2]).astype(BF16)
        turned = bv[2 * q:2 * q + 2, :ns].reshape(128, 128).T
        turned = jnp.concatenate([turned[:rows], turned[rows:]], axis=1)
        masks = (iota((ny, 256), 0) == place[0:1]).astype(BF16)
        masked = jnp.concatenate([turned * masks[b:b + 1] for b in range(ny)], axis=0)
        got = nt(masked, spread).reshape(ny, rows, 128)
        mv[...] = got if q == 0 else mv[...] + got

    keep = 1.0 - harvest
    zero = jnp.zeros((8, 128), F32)

    def block(lb, carry):
        sums, gone = carry
        cols = pl.ds(pl.multiple_of(lb * 128, 128), 128)
        new_sums, new_gone = [], []
        for il in range(il_n):
            tot, na, stay = zero, zero, zero
            for j in range(TYPES):
                m = jnp.broadcast_to(mv[lb, il * TYPES + j:il * TYPES + j + 1, :], (8, 128))
                term = m * stock[j, :, cols]
                tot = tot + term
                if j % il_n == il:
                    stay = jnp.where(x == j // il_n, term, stay)
                na = na + m * jnp.broadcast_to(areav[j:j + 1, cols], (8, 128))
            moved = tot - stay
            ns_i = stay + keep * moved
            new_sums.append(sums[il] + ns_i)
            new_gone.append(gone[il] + harvest * moved)
            snd[:, il, cols] = ns_i / na
            snd_a[il:il + 1, cols] = na[0:1]
        return tuple(new_sums), tuple(new_gone)

    zeros = (zero,) * il_n
    sums, gone = lax.fori_loop(0, ny, block, (zeros, zeros))

    word = zero
    for il in range(il_n):
        word = jnp.where(lane8 == row8 * il_n + il, jnp.sum(sums[il], axis=1, keepdims=True), word)
        word = jnp.where(lane8 == 8 * il_n + il, jnp.sum(gone[il], axis=1, keepdims=True), word)
    word = jnp.sum(word, axis=0, keepdims=True)
    red0[...] = word
    rc = []
    for o in far_s:
        t, to = dev_s(o)
        rc.append(send(red0, red1.at[me], r1_s.at[o], r1_r.at[o], to))
    red1[pl.ds(me, 1)] = word.reshape(1, 1, 128)
    ocp = []
    for o in far_x:
        t, to = dev_x(o)
        ocp.append(send(snd_a, rcv_a.at[x], a_s.at[o], a_r.at[o], to))
        ocp.append(send(snd.at[pl.ds(2 * t, 2)], rcv.at[x], o_s.at[o], o_r.at[o], to))

    rcv[pl.ds(x, 1)] = snd[pl.ds(2 * x, 2)].reshape(1, 2, il_n, owned)
    rcv_a[pl.ds(x, 1)] = snd_a[...].reshape(1, il_n, owned)
    for cp in rc:
        cp.wait_recv()
    tot = red1[0]
    for s in range(1, ns):
        tot = tot + red1[s]
    red2[...] = tot
    rc = []
    for o in far_yx:
        to = dev_yx(o)
        rc.append(send(red2, red3.at[y * nx + x], r2_s.at[o], r2_r.at[o], to))
    red3[pl.ds(y * nx + x, 1)] = tot.reshape(1, 1, 128)

    for cp in ocp:
        cp.wait_recv()
    run = None
    for i in range(TYPES):
        xs, il = i // il_n, i % il_n
        r = rcv_a[xs, il:il + 1, :]
        run = r if run is None else run + r
        out_cum[i:i + 1, :] = run
        for q in range(2):
            out_dens[q, i:i + 1, :] = rcv[xs, q, il:il + 1, :]
    out_cum[...] = out_cum[...] / run

    for cp in rc:
        cp.wait_recv()
    lane1 = iota((1, 128), 1)
    mean = [jnp.zeros((1, 128), F32)] * 2
    rem = jnp.zeros((1, 128), F32)
    for xs in range(nx):
        tot = red3[xs]
        for s in range(1, ny):
            tot = tot + red3[s * nx + xs]
        tot = tot / cells
        here = lane1 // il_n == xs
        rem = jnp.where(here, pltpu.roll(tot, 128 - 8 * il_n + xs * il_n, 1), rem)
        for q in range(2):
            away = lax.rem(128 + (xs - q) * il_n - 2 * il_n * x, 128)
            mean[q] = jnp.where(here, pltpu.roll(tot, away, 1), mean[q])
    out_rem[...] = rem[:, :TYPES]
    for q in range(2):
        out_mean[q:q + 1, :] = mean[q][:, :TYPES]
    for cp in sends:
        cp.wait_send()


def solution(mesh):
    nx = mesh.shape["pool"]
    nc = 2
    ncell = mesh.shape["cell"]
    nz = ny = int(round((ncell // nc) ** 0.5))
    finer = Mesh(mesh.devices.reshape(nz, ny, nc, nx), ("z", "y", "core", "pool"))
    ns = nz * nc
    half_n = 64 // ns
    owned = 128 * ny
    rows = 256 // nx
    il_n = TYPES // nx
    groups = ns * ny
    dims = (nz, ny, nc, nx, float(ncell * owned))
    any_, vm = pl.BlockSpec(memory_space=pl.ANY), pl.BlockSpec(memory_space=pltpu.VMEM)
    hbm = pl.BlockSpec(memory_space=pltpu.HBM)
    dma = pltpu.SemaphoreType.DMA

    def body(fractions, order, density, area, harvest):
        scratch = [
            pltpu.VMEM((2 * rows, owned), BF16),
            pltpu.VMEM((ny, 128), I32),
            pltpu.VMEM((TYPES, owned), F32),
            pltpu.SMEM((2,), F32),
            pltpu.VMEM((8, 128), F32),
            pltpu.VMEM((nx, 8, 128), F32),
            pltpu.VMEM((2 * nx, TYPES, owned), F32),
            pltpu.VMEM((TYPES, 2 * nx, owned), F32),
            pltpu.VMEM((ns, ny + 1, half_n, 128), BF16),
            pltpu.VMEM((ny + 1, ns + 1, half_n, 128), BF16),
            pltpu.VMEM((ny, ns + 1, half_n, 128), BF16),
            pltpu.VMEM((ny, rows, 128), F32),
            pltpu.VMEM((2 * nx, il_n, owned), F32),
            pltpu.VMEM((il_n, owned), F32),
            pltpu.VMEM((nx, 2, il_n, owned), F32),
            pltpu.VMEM((nx, il_n, owned), F32),
            pltpu.VMEM((1, 128), F32),
            pltpu.VMEM((ns, 1, 128), F32),
            pltpu.VMEM((1, 128), F32),
            pltpu.VMEM((ny * nx, 1, 128), F32),
            dma((6,)),
        ]
        for n in (nx, nx, ns, ny, nx, nx, ns, ny * nx):
            scratch += [dma((n,)), dma((n,))]
        results = pl.pallas_call(
            functools.partial(kernel, dims),
            out_shape=(
                jax.ShapeDtypeStruct((2, TYPES, owned), F32),
                jax.ShapeDtypeStruct((TYPES, owned), F32),
                jax.ShapeDtypeStruct((2, TYPES), F32),
                jax.ShapeDtypeStruct((1, TYPES), F32),
            ),
            in_specs=[hbm] * 5,
            out_specs=(vm, vm, vm, vm),
            scratch_shapes=scratch,
            compiler_params=pltpu.CompilerParams(collective_id=0, has_side_effects=True, vmem_limit_bytes=VMEM_LIMIT),
        )(*(pltpu.with_memory_space_constraint(a, pltpu.HBM) for a in (fractions, order.reshape(ny, 128), density, area, harvest)))
        dens, cum, mean, rem = pl.pallas_call(
            hand_over,
            out_shape=tuple(jax.ShapeDtypeStruct(r.shape, r.dtype) for r in results),
            in_specs=[any_] * 4,
            out_specs=(hbm,) * 4,
            scratch_shapes=[dma((4,))],
            compiler_params=pltpu.CompilerParams(vmem_limit_bytes=VMEM_LIMIT),
        )(*results)
        return dens, cum, mean, rem.reshape(TYPES)

    cell = ("z", "y", "core")
    return jax.shard_map(
        body,
        mesh=finer,
        in_specs=(P(None, cell), P(cell), P("pool", None, cell), P(None, cell), P("pool")),
        out_specs=(P("pool", None, cell), P(None, cell), P("pool", None), P()),
        check_vma=False,
    )
```

```python
import functools

import jax
import jax.numpy as jnp
from jax import lax
from jax.experimental import pallas as pl
from jax.experimental.pallas import tpu as pltpu
from jax.sharding import Mesh
from jax.sharding import PartitionSpec as P

MESH = pl.DeviceIdType.MESH
F32, BF16, I32 = jnp.float32, jnp.bfloat16, jnp.int32
TYPES = 16
VMEM_LIMIT = 12 * 1024 * 1024


def nt(a, b):
    return lax.dot_general(a, b, (((1,), (1,)), ((), ())), preferred_element_type=F32)


def iota(shape, dim):
    return lax.broadcasted_iota(I32, shape, dim)


def hand_over(*refs):
    sem = refs[8]
    copies = [pltpu.make_async_copy(refs[i], refs[4 + i], sem.at[i]) for i in range(4)]
    for cp in copies:
        cp.start()
    for cp in copies:
        cp.wait()


def kernel(dims, frac, order, dens, area, harv, out_dens, out_cum, out_mean, out_rem,
           f2, ordv, areav, hsm, hs, hg, dg, stock, sd, av, bv,
           mv, snd, snd_a, rcv, rcv_a, red0, red1, red2, red3, lsem,
           d_s, d_r, h_s, h_r, s1_s, s1_r, s2_s, s2_r,
           o_s, o_r, a_s, a_r, r1_s, r1_r, r2_s, r2_r):
    nz, ny, nc, nx, cells = dims
    ns = nz * nc
    rank_n = 128 // ns
    half_n = rank_n // 2
    owned = 128 * ny
    rows = 256 // nx
    il_n = TYPES // nx
    pools = 2 * nx
    z, y, c, x = (lax.axis_index(a) for a in ("z", "y", "core", "pool"))
    me = z * nc + c

    def dev_s(o):
        t = lax.rem(me + o, ns)
        return t, (t // nc, y, lax.rem(t, nc), x)

    def dev_y(o):
        t = lax.rem(y + o, ny)
        return t, (z, t, c, x)

    def dev_x(o):
        t = lax.rem(x + o, nx)
        return t, (z, y, c, t)

    def dev_yx(o):
        return z, lax.rem(y + o // nx, ny), c, lax.rem(x + o % nx, nx)

    local = [
        pltpu.make_async_copy(order, ordv, lsem.at[0]),
        pltpu.make_async_copy(frac.at[pl.ds(pl.multiple_of(x * rows, rows), rows), :], f2.at[pl.ds(0, rows), :], lsem.at[1]),
        pltpu.make_async_copy(frac.at[pl.ds(pl.multiple_of(x * rows, rows), rows), :], f2.at[pl.ds(rows, rows), :], lsem.at[2]),
        pltpu.make_async_copy(area, areav, lsem.at[3]),
        pltpu.make_async_copy(dens, dg.at[pl.ds(2 * x, 2)], lsem.at[4]),
        pltpu.make_async_copy(harv, hsm, lsem.at[5]),
    ]
    for cp in local:
        cp.start()

    barrier = pltpu.get_barrier_semaphore()
    peers = [dev_x(o)[1] for o in range(1, nx)]
    peers += [dev_y(o)[1] for o in range(1, ny)]
    peers += [dev_s(o)[1] for o in range(1, ns)]
    for p in peers:
        pl.semaphore_signal(barrier, inc=1, device_id=p, device_id_type=MESH)

    local[0].wait()
    ordr = ordv[...]
    dest = ordr // owned
    pos = lax.rem(ordr, owned)
    dz, dy, dc = dest // (ny * nc), lax.rem(dest // nc, ny), lax.rem(dest, nc)
    group = (dz * nc + dc) * ny + dy
    groups = ns * ny
    upper = (iota((128, 128), 0) < iota((128, 128), 1)).astype(BF16)
    ones = jnp.ones((128, 128), BF16)
    before = jnp.zeros((groups, 128), F32)
    ranks = []
    for b in range(ny):
        hot = iota((groups, 128), 0) == group[b:b + 1, :]
        hotb = hot.astype(BF16)
        count = jnp.dot(hotb, upper, preferred_element_type=F32) + before
        if b < ny - 1:
            before = before + jnp.dot(hotb, ones, preferred_element_type=F32)
        ranks.append(jnp.sum(jnp.where(hot, count, 0.0), axis=0, keepdims=True))
    rank = jnp.concatenate(ranks, axis=0).astype(I32)
    part = rank // half_n
    sub = lax.rem(rank, half_n)

    home = dz * nc + dc
    lane_of = part * 64 + lax.rem(me + dy, ns) * half_n + sub
    hi = (pos // 128).astype(F32)
    lo = lax.rem(pos, 128).astype(F32)
    digit = lax.rem(iota((ns * half_n, 128), 0), half_n)
    owner = iota((ns * half_n, 128), 0) // half_n
    left, right = [], []
    for b in range(ny):
        r = slice(b, b + 1)
        value = jnp.where(digit == 0, hi[r], jnp.where(digit == 1, lo[r], 0.0))
        left.append(jnp.where(owner == home[r], value, 0.0).astype(BF16))
        right.append((iota((128, 128), 0) == lane_of[r]).astype(BF16))
    placed = nt(jnp.concatenate(left, axis=1), jnp.concatenate(right, axis=1))
    sd[:, ny] = placed.astype(BF16).reshape(ns, half_n, 128)

    sends = []

    def send(src, dst, ss, rs, to):
        cp = pltpu.make_async_remote_copy(src_ref=src, dst_ref=dst, send_sem=ss, recv_sem=rs,
                                          device_id=to, device_id_type=MESH)
        cp.start()
        sends.append(cp)
        return cp

    far_s = sorted(range(1, ns), key=lambda o: -min(o, ns - o))
    far_y = sorted(range(1, ny), key=lambda o: -min(o, ny - o))
    far_yx = sorted(range(1, ny * nx), key=lambda o: -min(o // nx, ny - o // nx) - min(o % nx, nx - o % nx))
    near_y = far_y[::-1]
    slot = {o: 1 + near_y.index(o) for o in near_y}
    far_x = sorted(range(1, nx), key=lambda o: -min(o, nx - o))

    key = group * half_n + sub
    rho = groups * half_n
    local[1].wait()
    local[2].wait()
    halves = []
    for h in range(2):
        keyh = jnp.where(part == h, key, -1)
        hots = [(iota((rho, 128), 0) == keyh[b:b + 1, :]).astype(BF16) for b in range(ny)]
        halves.append(nt(jnp.concatenate(hots, axis=1), f2[...]))
    lanes = iota((rho, 128), 1)
    moved_cols = jnp.where(lanes < rows, halves[0], halves[1]).astype(BF16)
    sd[:, :ny] = moved_cols.reshape(ns, ny, half_n, 128)

    local[5].wait()
    row8, lane8 = iota((8, 128), 0), iota((8, 128), 1)
    hs[...] = jnp.where(row8 == 2 * x, hsm[0], jnp.where(row8 == 2 * x + 1, hsm[1], 0.0))

    pl.semaphore_wait(barrier, len(peers))
    s1 = []
    for o in far_s:
        t, to = dev_s(o)
        s1.append(send(sd.at[t], av.at[:, me], s1_s.at[o], s1_r.at[o], to))
    dcp, hcp = [], []
    for o in far_x:
        t, to = dev_x(o)
        hcp.append(send(hs, hg.at[x], h_s.at[o], h_r.at[o], to))
        dcp.append(send(dens, dg.at[pl.ds(2 * x, 2)], d_s.at[o], d_r.at[o], to))
    av[:, pl.ds(me, 1)] = sd[pl.ds(me, 1)].reshape(ny + 1, 1, half_n, 128)
    hg[pl.ds(x, 1)] = hs[...].reshape(1, 8, 128)

    shape3 = (ny, half_n, 128)
    source = lax.rem(lax.rem(iota(shape3, 2), 64) // half_n + ns - iota(shape3, 0), ns)
    placed = jnp.zeros(shape3, F32)
    for o in [0] + far_s[::-1]:
        src = lax.rem(me + ns - o, ns)
        if o:
            s1[far_s.index(o)].wait_recv()
        placed = jnp.where(source == src, av[ny, pl.ds(src, 1)].astype(F32), placed)
    av[:ny, ns] = placed.astype(BF16)
    s2 = []
    for o in near_y:
        t, to = dev_y(o)
        s2.append(send(av.at[t], bv.at[slot[o]], s2_s.at[o], s2_r.at[o], to))
    bv[0:1] = av[pl.ds(y, 1)]

    for cp in hcp:
        cp.wait_recv()
    harvest = hg[0]
    for s in range(1, nx):
        harvest = harvest + hg[s]
    local[3].wait()
    local[4].wait()
    for cp in dcp:
        cp.wait_recv()
    for j in range(TYPES):
        stock[j] = dg[:, j, :] * areav[j:j + 1, :]

    low = iota((2, 128), 1) < 64
    same = lax.rem(iota((2, 128), 1), 64) < 64 - half_n * y
    for q in range(ny // 2):
        rolled = []
        for k in (2 * q, 2 * q + 1):
            for o, cp in zip(near_y, s2):
                if slot[o] == k:
                    cp.wait_recv()
            digits = bv[k, ns].astype(F32)[0:2]
            rolled.append((pltpu.roll(digits, 128 - half_n * y, 1), pltpu.roll(digits, 64 - half_n * y, 1)))
        (a1, a2), (b1, b2) = rolled
        firsts = jnp.where(low, jnp.where(same, a1, a2), jnp.where(same, b2, b1))
        seconds = jnp.where(low, jnp.where(same, a2, a1), jnp.where(same, b1, b2))
        place = jnp.concatenate([firsts, seconds], axis=1).astype(I32)
        spread = (iota((128, 256), 0) == place[1:2]).astype(BF16)
        turned = bv[2 * q:2 * q + 2, :ns].reshape(128, 128).T
        turned = jnp.concatenate([turned[:rows], turned[rows:]], axis=1)
        masks = (iota((ny, 256), 0) == place[0:1]).astype(BF16)
        masked = jnp.concatenate([turned * masks[b:b + 1] for b in range(ny)], axis=0)
        got = nt(masked, spread).reshape(ny, rows, 128)
        mv[...] = got if q == 0 else mv[...] + got

    keep = 1.0 - harvest
    zero = jnp.zeros((8, 128), F32)

    def block(lb, carry):
        sums, gone = carry
        cols = pl.ds(pl.multiple_of(lb * 128, 128), 128)
        new_sums, new_gone = [], []
        for il in range(il_n):
            tot, na, stay = zero, zero, zero
            for j in range(TYPES):
                m = jnp.broadcast_to(mv[lb, il * TYPES + j:il * TYPES + j + 1, :], (8, 128))
                term = m * stock[j, :, cols]
                tot = tot + term
                if j % il_n == il:
                    stay = jnp.where(x == j // il_n, term, stay)
                na = na + m * jnp.broadcast_to(areav[j:j + 1, cols], (8, 128))
            moved = tot - stay
            ns_i = stay + keep * moved
            new_sums.append(sums[il] + ns_i)
            new_gone.append(gone[il] + harvest * moved)
            snd[:, il, cols] = ns_i / na
            snd_a[il:il + 1, cols] = na[0:1]
        return tuple(new_sums), tuple(new_gone)

    zeros = (zero,) * il_n
    sums, gone = lax.fori_loop(0, ny, block, (zeros, zeros))

    word = zero
    for il in range(il_n):
        word = jnp.where(lane8 == row8 * il_n + il, jnp.sum(sums[il], axis=1, keepdims=True), word)
        word = jnp.where(lane8 == 8 * il_n + il, jnp.sum(gone[il], axis=1, keepdims=True), word)
    word = jnp.sum(word, axis=0, keepdims=True)
    red0[...] = word
    rc = []
    for o in far_s:
        t, to = dev_s(o)
        rc.append(send(red0, red1.at[me], r1_s.at[o], r1_r.at[o], to))
    red1[pl.ds(me, 1)] = word.reshape(1, 1, 128)
    ocp = []
    for o in far_x:
        t, to = dev_x(o)
        ocp.append(send(snd_a, rcv_a.at[x], a_s.at[o], a_r.at[o], to))
        ocp.append(send(snd.at[pl.ds(2 * t, 2)], rcv.at[x], o_s.at[o], o_r.at[o], to))

    rcv[pl.ds(x, 1)] = snd[pl.ds(2 * x, 2)].reshape(1, 2, il_n, owned)
    rcv_a[pl.ds(x, 1)] = snd_a[...].reshape(1, il_n, owned)
    for cp in rc:
        cp.wait_recv()
    tot = red1[0]
    for s in range(1, ns):
        tot = tot + red1[s]
    red2[...] = tot
    rc = []
    for o in far_yx:
        to = dev_yx(o)
        rc.append(send(red2, red3.at[y * nx + x], r2_s.at[o], r2_r.at[o], to))
    red3[pl.ds(y * nx + x, 1)] = tot.reshape(1, 1, 128)

    for cp in ocp:
        cp.wait_recv()
    run = None
    for i in range(TYPES):
        xs, il = i // il_n, i % il_n
        r = rcv_a[xs, il:il + 1, :]
        run = r if run is None else run + r
        out_cum[i:i + 1, :] = run
        for q in range(2):
            out_dens[q, i:i + 1, :] = rcv[xs, q, il:il + 1, :]
    out_cum[...] = out_cum[...] / run

    for cp in rc:
        cp.wait_recv()
    lane1 = iota((1, 128), 1)
    mean = [jnp.zeros((1, 128), F32)] * 2
    rem = jnp.zeros((1, 128), F32)
    for xs in range(nx):
        tot = red3[xs]
        for s in range(1, ny):
            tot = tot + red3[s * nx + xs]
        tot = tot / cells
        here = lane1 // il_n == xs
        rem = jnp.where(here, pltpu.roll(tot, 128 - 8 * il_n + xs * il_n, 1), rem)
        for q in range(2):
            away = lax.rem(128 + (xs - q) * il_n - 2 * il_n * x, 128)
            mean[q] = jnp.where(here, pltpu.roll(tot, away, 1), mean[q])
    out_rem[...] = rem[:, :TYPES]
    for q in range(2):
        out_mean[q:q + 1, :] = mean[q][:, :TYPES]
    for cp in sends:
        cp.wait_send()


def solution(mesh):
    nx = mesh.shape["pool"]
    nc = 2
    ncell = mesh.shape["cell"]
    nz = ny = int(round((ncell // nc) ** 0.5))
    finer = Mesh(mesh.devices.reshape(nz, ny, nc, nx), ("z", "y", "core", "pool"))
    ns = nz * nc
    half_n = 64 // ns
    owned = 128 * ny
    rows = 256 // nx
    il_n = TYPES // nx
    groups = ns * ny
    dims = (nz, ny, nc, nx, float(ncell * owned))
    any_, vm = pl.BlockSpec(memory_space=pl.ANY), pl.BlockSpec(memory_space=pltpu.VMEM)
    hbm = pl.BlockSpec(memory_space=pltpu.HBM)
    dma = pltpu.SemaphoreType.DMA

    def body(fractions, order, density, area, harvest):
        scratch = [
            pltpu.VMEM((2 * rows, owned), BF16),
            pltpu.VMEM((ny, 128), I32),
            pltpu.VMEM((TYPES, owned), F32),
            pltpu.SMEM((2,), F32),
            pltpu.VMEM((8, 128), F32),
            pltpu.VMEM((nx, 8, 128), F32),
            pltpu.VMEM((2 * nx, TYPES, owned), F32),
            pltpu.VMEM((TYPES, 2 * nx, owned), F32),
            pltpu.VMEM((ns, ny + 1, half_n, 128), BF16),
            pltpu.VMEM((ny + 1, ns + 1, half_n, 128), BF16),
            pltpu.VMEM((ny, ns + 1, half_n, 128), BF16),
            pltpu.VMEM((ny, rows, 128), F32),
            pltpu.VMEM((2 * nx, il_n, owned), F32),
            pltpu.VMEM((il_n, owned), F32),
            pltpu.VMEM((nx, 2, il_n, owned), F32),
            pltpu.VMEM((nx, il_n, owned), F32),
            pltpu.VMEM((1, 128), F32),
            pltpu.VMEM((ns, 1, 128), F32),
            pltpu.VMEM((1, 128), F32),
            pltpu.VMEM((ny * nx, 1, 128), F32),
            dma((6,)),
        ]
        for n in (nx, nx, ns, ny, nx, nx, ns, ny * nx):
            scratch += [dma((n,)), dma((n,))]
        results = pl.pallas_call(
            functools.partial(kernel, dims),
            out_shape=(
                jax.ShapeDtypeStruct((2, TYPES, owned), F32),
                jax.ShapeDtypeStruct((TYPES, owned), F32),
                jax.ShapeDtypeStruct((2, TYPES), F32),
                jax.ShapeDtypeStruct((1, TYPES), F32),
            ),
            in_specs=[hbm] * 5,
            out_specs=(vm, vm, vm, vm),
            scratch_shapes=scratch,
            compiler_params=pltpu.CompilerParams(collective_id=0, has_side_effects=True, vmem_limit_bytes=VMEM_LIMIT),
        )(*(pltpu.with_memory_space_constraint(a, pltpu.HBM) for a in (fractions, order.reshape(ny, 128), density, area, harvest)))
        dens, cum, mean, rem = pl.pallas_call(
            hand_over,
            out_shape=tuple(jax.ShapeDtypeStruct(r.shape, r.dtype) for r in results),
            in_specs=[any_] * 4,
            out_specs=(hbm,) * 4,
            scratch_shapes=[dma((4,))],
            compiler_params=pltpu.CompilerParams(vmem_limit_bytes=VMEM_LIMIT),
        )(*results)
        return dens, cum, mean, rem.reshape(TYPES)

    cell = ("z", "y", "core")
    return jax.shard_map(
        body,
        mesh=finer,
        in_specs=(P(None, cell), P(cell), P("pool", None, cell), P(None, cell), P("pool")),
        out_specs=(P("pool", None, cell), P(None, cell), P("pool", None), P()),
        check_vma=False,
    )
```

```python
import functools

import jax
import jax.numpy as jnp
from jax import lax
from jax.experimental import pallas as pl
from jax.experimental.pallas import tpu as pltpu
from jax.sharding import Mesh
from jax.sharding import PartitionSpec as P

MESH = pl.DeviceIdType.MESH
F32, BF16, I32 = jnp.float32, jnp.bfloat16, jnp.int32
TYPES = 16
VMEM_LIMIT = 12 * 1024 * 1024


def nt(a, b):
    return lax.dot_general(a, b, (((1,), (1,)), ((), ())), preferred_element_type=F32)


def nearness(o, n):
    return jnp.where(2 * o < n, jnp.maximum(2 * o - 1, 0), jnp.where(2 * o == n, n - 1, 2 * (n - o)))


def near_slot(o, n):
    return max(2 * o - 1, 0) if 2 * o < n else n - 1 if 2 * o == n else 2 * (n - o)


def iota(shape, dim):
    return lax.broadcasted_iota(I32, shape, dim)


def hand_over(*refs):
    sem = refs[8]
    copies = [pltpu.make_async_copy(refs[i], refs[4 + i], sem.at[i]) for i in range(4)]
    for cp in copies:
        cp.start()
    for cp in copies:
        cp.wait()


def kernel(dims, frac, order, dens, area, harv, out_dens, out_cum, out_mean, out_rem,
           f2, ordv, areav, hsm, hs, hg, dg, stock, sd, av, bv,
           mv, snd, snd_a, rcv, rcv_a, red0, red1, red2, red3, lsem,
           d_s, d_r, h_s, h_r, s1_s, s1_r, s2_s, s2_r, s2a_s, s2a_r,
           o_s, o_r, a_s, a_r, r1_s, r1_r, r2_s, r2_r):
    nz, ny, nc, nx, cells = dims
    ns = nz * nc
    rank_n = 128 // ns
    half_n = rank_n // 2
    owned = 128 * ny
    rows = 256 // nx
    il_n = TYPES // nx
    pools = 2 * nx
    z, y, c, x = (lax.axis_index(a) for a in ("z", "y", "core", "pool"))
    me = z * nc + c

    def dev_s(o):
        t = lax.rem(me + o, ns)
        return t, (t // nc, y, lax.rem(t, nc), x)

    def dev_y(o):
        t = lax.rem(y + o, ny)
        return t, (z, t, c, x)

    def dev_x(o):
        t = lax.rem(x + o, nx)
        return t, (z, y, c, t)

    def dev_yx(o):
        return z, lax.rem(y + o // nx, ny), c, lax.rem(x + o % nx, nx)

    local = [
        pltpu.make_async_copy(order, ordv, lsem.at[0]),
        pltpu.make_async_copy(frac.at[pl.ds(pl.multiple_of(x * rows, rows), rows), :], f2.at[pl.ds(0, rows), :], lsem.at[1]),
        pltpu.make_async_copy(frac.at[pl.ds(pl.multiple_of(x * rows, rows), rows), :], f2.at[pl.ds(rows, rows), :], lsem.at[2]),
        pltpu.make_async_copy(area, areav, lsem.at[3]),
        pltpu.make_async_copy(dens, dg.at[pl.ds(2 * x, 2)], lsem.at[4]),
        pltpu.make_async_copy(harv, hsm, lsem.at[5]),
    ]
    for cp in local:
        cp.start()

    barrier = pltpu.get_barrier_semaphore()
    peers = [dev_s(o)[1] for o in sorted(range(1, ns), key=lambda o: -min(o, ns - o))]
    peers += [dev_y(o)[1] for o in sorted(range(1, ny), key=lambda o: -min(o, ny - o))]
    peers += [dev_x(o)[1] for o in range(1, nx)]
    for p in peers:
        pl.semaphore_signal(barrier, inc=1, device_id=p, device_id_type=MESH)

    local[0].wait()
    ordr = ordv[...]
    dest = ordr // owned
    pos = lax.rem(ordr, owned)
    dz, dy, dc = dest // (ny * nc), lax.rem(dest // nc, ny), lax.rem(dest, nc)
    group = (dz * nc + dc) * ny + dy
    groups = ns * ny
    upper = (iota((128, 128), 0) < iota((128, 128), 1)).astype(BF16)
    ones = jnp.ones((128, 128), BF16)
    before = jnp.zeros((groups, 128), F32)
    ranks = []
    for b in range(ny):
        hot = iota((groups, 128), 0) == group[b:b + 1, :]
        hotb = hot.astype(BF16)
        count = jnp.dot(hotb, upper, preferred_element_type=F32) + before
        if b < ny - 1:
            before = before + jnp.dot(hotb, ones, preferred_element_type=F32)
        ranks.append(jnp.sum(jnp.where(hot, count, 0.0), axis=0, keepdims=True))
    rank = jnp.concatenate(ranks, axis=0).astype(I32)
    part = rank // half_n
    sub = lax.rem(rank, half_n)

    home = dz * nc + dc
    lane_of = part * 64 + lax.rem(nearness(lax.rem(home + ns - me, ns), ns) + dy, ns) * half_n + sub
    hi = (pos // 128).astype(F32)
    lo = lax.rem(pos, 128).astype(F32)
    digit = lax.rem(iota((ns * half_n, 128), 0), half_n)
    owner = iota((ns * half_n, 128), 0) // half_n
    left, right = [], []
    for b in range(ny):
        r = slice(b, b + 1)
        value = jnp.where(digit == 0, hi[r], jnp.where(digit == 1, lo[r], 0.0))
        left.append(jnp.where(owner == home[r], value, 0.0).astype(BF16))
        right.append((iota((128, 128), 0) == lane_of[r]).astype(BF16))
    placed = nt(jnp.concatenate(left, axis=1), jnp.concatenate(right, axis=1))
    sd[:, ny] = placed.astype(BF16).reshape(ns, half_n, 128)

    sends = []

    def send(src, dst, ss, rs, to):
        cp = pltpu.make_async_remote_copy(src_ref=src, dst_ref=dst, send_sem=ss, recv_sem=rs,
                                          device_id=to, device_id_type=MESH)
        cp.start()
        sends.append(cp)
        return cp

    far_s = sorted(range(1, ns), key=lambda o: -min(o, ns - o))
    far_y = sorted(range(1, ny), key=lambda o: -min(o, ny - o))
    far_yx = sorted(range(1, ny * nx), key=lambda o: -min(o // nx, ny - o // nx) - min(o % nx, nx - o % nx))
    near_y = far_y[::-1]
    slot = {o: 1 + near_y.index(o) for o in near_y}
    far_x = sorted(range(1, nx), key=lambda o: -min(o, nx - o))

    key = group * half_n + sub
    rho = groups * half_n
    local[1].wait()
    local[2].wait()
    halves = []
    for h in range(2):
        keyh = jnp.where(part == h, key, -1)
        hots = [(iota((rho, 128), 0) == keyh[b:b + 1, :]).astype(BF16) for b in range(ny)]
        halves.append(nt(jnp.concatenate(hots, axis=1), f2[...]))
    lanes = iota((rho, 128), 1)
    moved_cols = jnp.where(lanes < rows, halves[0], halves[1]).astype(BF16)
    sd[:, :ny] = moved_cols.reshape(ns, ny, half_n, 128)

    local[5].wait()
    row8, lane8 = iota((8, 128), 0), iota((8, 128), 1)
    hs[...] = jnp.where(row8 == 2 * x, hsm[0], jnp.where(row8 == 2 * x + 1, hsm[1], 0.0))

    pl.semaphore_wait(barrier, len(peers))
    s1 = []
    for o in far_s[::-1]:
        t, to = dev_s(o)
        s1.append(send(sd.at[t], av.at[:, near_slot(o, ns)], s1_s.at[o], s1_r.at[o], to))
    s1 = s1[::-1]
    dcp, hcp = [], []
    for o in far_x:
        t, to = dev_x(o)
        hcp.append(send(hs, hg.at[x], h_s.at[o], h_r.at[o], to))
        dcp.append(send(dens, dg.at[pl.ds(2 * x, 2)], d_s.at[o], d_r.at[o], to))
    av[:, 0:1] = sd[pl.ds(me, 1)].reshape(ny + 1, 1, half_n, 128)
    hg[pl.ds(x, 1)] = hs[...].reshape(1, 8, 128)

    shape3 = (ny, half_n, 128)
    source = lax.rem(lax.rem(iota(shape3, 2), 64) // half_n + ns - iota(shape3, 0), ns)
    placed = jnp.zeros(shape3, F32)
    first, s2a, s2 = ns // 2, [], []
    for k, o in enumerate(sorted(range(ns), key=lambda o: near_slot(o, ns))):
        if o:
            s1[far_s.index(o)].wait_recv()
        placed = jnp.where(source == k, av[ny, k:k + 1].astype(F32), placed)
        if k == first - 1:
            for p in near_y:
                t, to = dev_y(p)
                s2a.append(send(av.at[t, pl.ds(0, first)], bv.at[slot[p], pl.ds(0, first)], s2a_s.at[p], s2a_r.at[p], to))
    av[:ny, ns] = placed.astype(BF16)
    for o in near_y:
        t, to = dev_y(o)
        s2.append(send(av.at[t, pl.ds(first, ns + 1 - first)], bv.at[slot[o], pl.ds(first, ns + 1 - first)], s2_s.at[o], s2_r.at[o], to))
    bv[0:1] = av[pl.ds(y, 1)]

    for cp in hcp:
        cp.wait_recv()
    harvest = hg[0]
    for s in range(1, nx):
        harvest = harvest + hg[s]
    local[3].wait()
    local[4].wait()
    for cp in dcp:
        cp.wait_recv()
    for j in range(TYPES):
        stock[j] = dg[:, j, :] * areav[j:j + 1, :]

    low = iota((2, 128), 1) < 64
    same = lax.rem(iota((2, 128), 1), 64) < 64 - half_n * y
    for q in range(ny // 2):
        rolled = []
        for k in (2 * q, 2 * q + 1):
            for o, ca, cp in zip(near_y, s2a, s2):
                if slot[o] == k:
                    ca.wait_recv()
                    cp.wait_recv()
            digits = bv[k, ns].astype(F32)[0:2]
            rolled.append((pltpu.roll(digits, 128 - half_n * y, 1), pltpu.roll(digits, 64 - half_n * y, 1)))
        (a1, a2), (b1, b2) = rolled
        firsts = jnp.where(low, jnp.where(same, a1, a2), jnp.where(same, b2, b1))
        seconds = jnp.where(low, jnp.where(same, a2, a1), jnp.where(same, b1, b2))
        place = jnp.concatenate([firsts, seconds], axis=1).astype(I32)
        spread = (iota((128, 256), 0) == place[1:2]).astype(BF16)
        turned = bv[2 * q:2 * q + 2, :ns].reshape(128, 128).T
        turned = jnp.concatenate([turned[:rows], turned[rows:]], axis=1)
        masks = (iota((ny, 256), 0) == place[0:1]).astype(BF16)
        masked = jnp.concatenate([turned * masks[b:b + 1] for b in range(ny)], axis=0)
        got = nt(masked, spread).reshape(ny, rows, 128)
        mv[...] = got if q == 0 else mv[...] + got

    keep = 1.0 - harvest
    zero = jnp.zeros((8, 128), F32)

    def block(lb, carry):
        sums, gone = carry
        cols = pl.ds(pl.multiple_of(lb * 128, 128), 128)
        new_sums, new_gone = [], []
        for il in range(il_n):
            tot, na, stay = zero, zero, zero
            for j in range(TYPES):
                m = jnp.broadcast_to(mv[lb, il * TYPES + j:il * TYPES + j + 1, :], (8, 128))
                term = m * stock[j, :, cols]
                tot = tot + term
                if j % il_n == il:
                    stay = jnp.where(x == j // il_n, term, stay)
                na = na + m * jnp.broadcast_to(areav[j:j + 1, cols], (8, 128))
            moved = tot - stay
            ns_i = stay + keep * moved
            new_sums.append(sums[il] + ns_i)
            new_gone.append(gone[il] + harvest * moved)
            snd[:, il, cols] = ns_i / na
            snd_a[il:il + 1, cols] = na[0:1]
        return tuple(new_sums), tuple(new_gone)

    zeros = (zero,) * il_n
    sums, gone = lax.fori_loop(0, ny, block, (zeros, zeros))

    word = zero
    for il in range(il_n):
        word = jnp.where(lane8 == row8 * il_n + il, jnp.sum(sums[il], axis=1, keepdims=True), word)
        word = jnp.where(lane8 == 8 * il_n + il, jnp.sum(gone[il], axis=1, keepdims=True), word)
    word = jnp.sum(word, axis=0, keepdims=True)
    red0[...] = word
    rc = []
    for o in far_s:
        t, to = dev_s(o)
        rc.append(send(red0, red1.at[me], r1_s.at[o], r1_r.at[o], to))
    red1[pl.ds(me, 1)] = word.reshape(1, 1, 128)
    ocp = []
    for o in far_x:
        t, to = dev_x(o)
        ocp.append(send(snd_a, rcv_a.at[x], a_s.at[o], a_r.at[o], to))
        ocp.append(send(snd.at[pl.ds(2 * t, 2)], rcv.at[x], o_s.at[o], o_r.at[o], to))

    rcv[pl.ds(x, 1)] = snd[pl.ds(2 * x, 2)].reshape(1, 2, il_n, owned)
    rcv_a[pl.ds(x, 1)] = snd_a[...].reshape(1, il_n, owned)
    for cp in rc:
        cp.wait_recv()
    tot = red1[0]
    for s in range(1, ns):
        tot = tot + red1[s]
    red2[...] = tot
    rc = []
    for o in far_yx:
        to = dev_yx(o)
        rc.append(send(red2, red3.at[y * nx + x], r2_s.at[o], r2_r.at[o], to))
    red3[pl.ds(y * nx + x, 1)] = tot.reshape(1, 1, 128)

    for cp in ocp:
        cp.wait_recv()
    run = None
    for i in range(TYPES):
        xs, il = i // il_n, i % il_n
        r = rcv_a[xs, il:il + 1, :]
        run = r if run is None else run + r
        out_cum[i:i + 1, :] = run
        for q in range(2):
            out_dens[q, i:i + 1, :] = rcv[xs, q, il:il + 1, :]
    out_cum[...] = out_cum[...] / run

    for cp in rc:
        cp.wait_recv()
    lane1 = iota((1, 128), 1)
    mean = [jnp.zeros((1, 128), F32)] * 2
    rem = jnp.zeros((1, 128), F32)
    for xs in range(nx):
        tot = red3[xs]
        for s in range(1, ny):
            tot = tot + red3[s * nx + xs]
        tot = tot / cells
        here = lane1 // il_n == xs
        rem = jnp.where(here, pltpu.roll(tot, 128 - 8 * il_n + xs * il_n, 1), rem)
        for q in range(2):
            away = lax.rem(128 + (xs - q) * il_n - 2 * il_n * x, 128)
            mean[q] = jnp.where(here, pltpu.roll(tot, away, 1), mean[q])
    out_rem[...] = rem[:, :TYPES]
    for q in range(2):
        out_mean[q:q + 1, :] = mean[q][:, :TYPES]
    for cp in sends:
        cp.wait_send()


def solution(mesh):
    nx = mesh.shape["pool"]
    nc = 2
    ncell = mesh.shape["cell"]
    nz = ny = int(round((ncell // nc) ** 0.5))
    finer = Mesh(mesh.devices.reshape(nz, ny, nc, nx), ("z", "y", "core", "pool"))
    ns = nz * nc
    half_n = 64 // ns
    owned = 128 * ny
    rows = 256 // nx
    il_n = TYPES // nx
    groups = ns * ny
    dims = (nz, ny, nc, nx, float(ncell * owned))
    any_, vm = pl.BlockSpec(memory_space=pl.ANY), pl.BlockSpec(memory_space=pltpu.VMEM)
    hbm = pl.BlockSpec(memory_space=pltpu.HBM)
    dma = pltpu.SemaphoreType.DMA

    def body(fractions, order, density, area, harvest):
        scratch = [
            pltpu.VMEM((2 * rows, owned), BF16),
            pltpu.VMEM((ny, 128), I32),
            pltpu.VMEM((TYPES, owned), F32),
            pltpu.SMEM((2,), F32),
            pltpu.VMEM((8, 128), F32),
            pltpu.VMEM((nx, 8, 128), F32),
            pltpu.VMEM((2 * nx, TYPES, owned), F32),
            pltpu.VMEM((TYPES, 2 * nx, owned), F32),
            pltpu.VMEM((ns, ny + 1, half_n, 128), BF16),
            pltpu.VMEM((ny + 1, ns + 1, half_n, 128), BF16),
            pltpu.VMEM((ny, ns + 1, half_n, 128), BF16),
            pltpu.VMEM((ny, rows, 128), F32),
            pltpu.VMEM((2 * nx, il_n, owned), F32),
            pltpu.VMEM((il_n, owned), F32),
            pltpu.VMEM((nx, 2, il_n, owned), F32),
            pltpu.VMEM((nx, il_n, owned), F32),
            pltpu.VMEM((1, 128), F32),
            pltpu.VMEM((ns, 1, 128), F32),
            pltpu.VMEM((1, 128), F32),
            pltpu.VMEM((ny * nx, 1, 128), F32),
            dma((6,)),
        ]
        for n in (nx, nx, ns, ny, ny, nx, nx, ns, ny * nx):
            scratch += [dma((n,)), dma((n,))]
        results = pl.pallas_call(
            functools.partial(kernel, dims),
            out_shape=(
                jax.ShapeDtypeStruct((2, TYPES, owned), F32),
                jax.ShapeDtypeStruct((TYPES, owned), F32),
                jax.ShapeDtypeStruct((2, TYPES), F32),
                jax.ShapeDtypeStruct((1, TYPES), F32),
            ),
            in_specs=[hbm] * 5,
            out_specs=(vm, vm, vm, vm),
            scratch_shapes=scratch,
            compiler_params=pltpu.CompilerParams(collective_id=0, has_side_effects=True, vmem_limit_bytes=VMEM_LIMIT),
        )(*(pltpu.with_memory_space_constraint(a, pltpu.HBM) for a in (fractions, order.reshape(ny, 128), density, area, harvest)))
        dens, cum, mean, rem = pl.pallas_call(
            hand_over,
            out_shape=tuple(jax.ShapeDtypeStruct(r.shape, r.dtype) for r in results),
            in_specs=[any_] * 4,
            out_specs=(hbm,) * 4,
            scratch_shapes=[dma((4,))],
            compiler_params=pltpu.CompilerParams(vmem_limit_bytes=VMEM_LIMIT),
        )(*results)
        return dens, cum, mean, rem.reshape(TYPES)

    cell = ("z", "y", "core")
    return jax.shard_map(
        body,
        mesh=finer,
        in_specs=(P(None, cell), P(cell), P("pool", None, cell), P(None, cell), P("pool")),
        out_specs=(P("pool", None, cell), P(None, cell), P("pool", None), P()),
        check_vma=False,
    )
```

```python
import functools

import jax
import jax.numpy as jnp
from jax import lax
from jax.experimental import pallas as pl
from jax.experimental.pallas import tpu as pltpu
from jax.sharding import Mesh
from jax.sharding import PartitionSpec as P

MESH = pl.DeviceIdType.MESH
F32, BF16, I32 = jnp.float32, jnp.bfloat16, jnp.int32
TYPES = 16
VMEM_LIMIT = 12 * 1024 * 1024


def nt(a, b):
    return lax.dot_general(a, b, (((1,), (1,)), ((), ())), preferred_element_type=F32)


def nearness(o, n):
    return jnp.where(2 * o < n, jnp.maximum(2 * o - 1, 0), jnp.where(2 * o == n, n - 1, 2 * (n - o)))


def near_slot(o, n):
    return max(2 * o - 1, 0) if 2 * o < n else n - 1 if 2 * o == n else 2 * (n - o)


def iota(shape, dim):
    return lax.broadcasted_iota(I32, shape, dim)


def hand_over(*refs):
    sem = refs[8]
    copies = [pltpu.make_async_copy(refs[i], refs[4 + i], sem.at[i]) for i in range(4)]
    for cp in copies:
        cp.start()
    for cp in copies:
        cp.wait()


def kernel(dims, frac, order, dens, area, harv, out_dens, out_cum, out_mean, out_rem,
           f2, ordv, areav, hsm, hs, hg, dg, stock, sd, av, bv,
           mv, snd, snd_a, rcv, rcv_a, red0, red1, red2, red3, lsem,
           d_s, d_r, h_s, h_r, s1_s, s1_r, s2_s, s2_r, s2a_s, s2a_r,
           o_s, o_r, a_s, a_r, r1_s, r1_r, r2_s, r2_r):
    nz, ny, nc, nx, cells = dims
    ns = nz * nc
    rank_n = 128 // ns
    half_n = rank_n // 2
    owned = 128 * ny
    rows = 256 // nx
    il_n = TYPES // nx
    pools = 2 * nx
    z, y, c, x = (lax.axis_index(a) for a in ("z", "y", "core", "pool"))
    me = z * nc + c

    def dev_s(o):
        t = lax.rem(me + o, ns)
        return t, (t // nc, y, lax.rem(t, nc), x)

    def dev_y(o):
        t = lax.rem(y + o, ny)
        return t, (z, t, c, x)

    def dev_x(o):
        t = lax.rem(x + o, nx)
        return t, (z, y, c, t)

    def dev_yx(o):
        return z, lax.rem(y + o // nx, ny), c, lax.rem(x + o % nx, nx)

    local = [
        pltpu.make_async_copy(order, ordv, lsem.at[0]),
        pltpu.make_async_copy(frac.at[pl.ds(pl.multiple_of(x * rows, rows), rows), :], f2.at[pl.ds(0, rows), :], lsem.at[1]),
        pltpu.make_async_copy(frac.at[pl.ds(pl.multiple_of(x * rows, rows), rows), :], f2.at[pl.ds(rows, rows), :], lsem.at[2]),
        pltpu.make_async_copy(area, areav, lsem.at[3]),
        pltpu.make_async_copy(dens, dg.at[pl.ds(2 * x, 2)], lsem.at[4]),
        pltpu.make_async_copy(harv, hsm, lsem.at[5]),
    ]
    for cp in local:
        cp.start()

    barrier = pltpu.get_barrier_semaphore()
    peers = [dev_s(o)[1] for o in sorted(range(1, ns), key=lambda o: -min(o, ns - o))]
    peers += [dev_y(o)[1] for o in sorted(range(1, ny), key=lambda o: -min(o, ny - o))]
    peers += [dev_x(o)[1] for o in range(1, nx)]
    for p in peers:
        pl.semaphore_signal(barrier, inc=1, device_id=p, device_id_type=MESH)

    local[0].wait()
    ordr = ordv[...]
    dest = ordr // owned
    pos = lax.rem(ordr, owned)
    dz, dy, dc = dest // (ny * nc), lax.rem(dest // nc, ny), lax.rem(dest, nc)
    group = (dz * nc + dc) * ny + dy
    groups = ns * ny
    upper = (iota((128, 128), 0) < iota((128, 128), 1)).astype(BF16)
    ones = jnp.ones((128, 128), BF16)
    before = jnp.zeros((groups, 128), F32)
    ranks = []
    for b in range(ny):
        hot = iota((groups, 128), 0) == group[b:b + 1, :]
        hotb = hot.astype(BF16)
        count = jnp.dot(hotb, upper, preferred_element_type=F32) + before
        if b < ny - 1:
            before = before + jnp.dot(hotb, ones, preferred_element_type=F32)
        ranks.append(jnp.sum(jnp.where(hot, count, 0.0), axis=0, keepdims=True))
    rank = jnp.concatenate(ranks, axis=0).astype(I32)
    part = rank // half_n
    sub = lax.rem(rank, half_n)

    home = dz * nc + dc
    lane_of = part * 64 + lax.rem(nearness(lax.rem(home + ns - me, ns), ns) + dy, ns) * half_n + sub
    hi = (pos // 128).astype(F32)
    lo = lax.rem(pos, 128).astype(F32)
    digit = lax.rem(iota((ns * half_n, 128), 0), half_n)
    owner = iota((ns * half_n, 128), 0) // half_n
    left, right = [], []
    for b in range(ny):
        r = slice(b, b + 1)
        value = jnp.where(digit == 0, hi[r], jnp.where(digit == 1, lo[r], 0.0))
        left.append(jnp.where(owner == home[r], value, 0.0).astype(BF16))
        right.append((iota((128, 128), 0) == lane_of[r]).astype(BF16))
    placed = nt(jnp.concatenate(left, axis=1), jnp.concatenate(right, axis=1))
    sd[:, ny] = placed.astype(BF16).reshape(ns, half_n, 128)

    sends = []

    def send(src, dst, ss, rs, to):
        cp = pltpu.make_async_remote_copy(src_ref=src, dst_ref=dst, send_sem=ss, recv_sem=rs,
                                          device_id=to, device_id_type=MESH)
        cp.start()
        sends.append(cp)
        return cp

    far_s = sorted(range(1, ns), key=lambda o: -min(o, ns - o))
    far_y = sorted(range(1, ny), key=lambda o: -min(o, ny - o))
    far_yx = sorted(range(1, ny * nx), key=lambda o: -min(o // nx, ny - o // nx) - min(o % nx, nx - o % nx))
    near_y = far_y[::-1]
    slot = {o: 1 + near_y.index(o) for o in near_y}
    far_x = sorted(range(1, nx), key=lambda o: -min(o, nx - o))

    key = group * half_n + sub
    rho = groups * half_n
    local[1].wait()
    local[2].wait()
    halves = []
    for h in range(2):
        keyh = jnp.where(part == h, key, -1)
        hots = [(iota((rho, 128), 0) == keyh[b:b + 1, :]).astype(BF16) for b in range(ny)]
        halves.append(nt(jnp.concatenate(hots, axis=1), f2[...]))
    lanes = iota((rho, 128), 1)
    moved_cols = jnp.where(lanes < rows, halves[0], halves[1]).astype(BF16)
    sd[:, :ny] = moved_cols.reshape(ns, ny, half_n, 128)

    local[5].wait()
    row8, lane8 = iota((8, 128), 0), iota((8, 128), 1)
    hs[...] = jnp.where(row8 == 2 * x, hsm[0], jnp.where(row8 == 2 * x + 1, hsm[1], 0.0))

    pl.semaphore_wait(barrier, len(peers))
    s1 = []
    for o in far_s[::-1]:
        t, to = dev_s(o)
        s1.append(send(sd.at[t], av.at[:, near_slot(o, ns)], s1_s.at[o], s1_r.at[o], to))
    s1 = s1[::-1]
    dcp, hcp = [], []
    for o in far_x:
        t, to = dev_x(o)
        hcp.append(send(hs, hg.at[x], h_s.at[o], h_r.at[o], to))
        dcp.append(send(dens, dg.at[pl.ds(2 * x, 2)], d_s.at[o], d_r.at[o], to))
    av[:, 0:1] = sd[pl.ds(me, 1)].reshape(ny + 1, 1, half_n, 128)
    hg[pl.ds(x, 1)] = hs[...].reshape(1, 8, 128)

    shape3 = (ny, half_n, 128)
    source = lax.rem(lax.rem(iota(shape3, 2), 64) // half_n + ns - iota(shape3, 0), ns)
    placed = jnp.zeros(shape3, F32)
    first, s2a, s2 = ns // 2, [], []
    for k, o in enumerate(sorted(range(ns), key=lambda o: near_slot(o, ns))):
        if o:
            s1[far_s.index(o)].wait_recv()
        placed = jnp.where(source == k, av[ny, k:k + 1].astype(F32), placed)
        if k == first - 1:
            for p in near_y:
                t, to = dev_y(p)
                s2a.append(send(av.at[t, pl.ds(0, first)], bv.at[slot[p], pl.ds(0, first)], s2a_s.at[p], s2a_r.at[p], to))
    av[:ny, ns] = placed.astype(BF16)
    for o in near_y:
        t, to = dev_y(o)
        s2.append(send(av.at[t, pl.ds(first, ns + 1 - first)], bv.at[slot[o], pl.ds(first, ns + 1 - first)], s2_s.at[o], s2_r.at[o], to))
    bv[0:1] = av[pl.ds(y, 1)]

    for cp in hcp:
        cp.wait_recv()
    harvest = hg[0]
    for s in range(1, nx):
        harvest = harvest + hg[s]
    local[3].wait()
    local[4].wait()
    for cp in dcp:
        cp.wait_recv()
    for j in range(TYPES):
        stock[j] = dg[:, j, :] * areav[j:j + 1, :]

    low = iota((2, 128), 1) < 64
    same = lax.rem(iota((2, 128), 1), 64) < 64 - half_n * y
    for q in range(ny // 2):
        rolled = []
        for k in (2 * q, 2 * q + 1):
            for o, ca, cp in zip(near_y, s2a, s2):
                if slot[o] == k:
                    ca.wait_recv()
                    cp.wait_recv()
            digits = bv[k, ns].astype(F32)[0:2]
            rolled.append((pltpu.roll(digits, 128 - half_n * y, 1), pltpu.roll(digits, 64 - half_n * y, 1)))
        (a1, a2), (b1, b2) = rolled
        firsts = jnp.where(low, jnp.where(same, a1, a2), jnp.where(same, b2, b1))
        seconds = jnp.where(low, jnp.where(same, a2, a1), jnp.where(same, b1, b2))
        place = jnp.concatenate([firsts, seconds], axis=1).astype(I32)
        spread = (iota((128, 256), 0) == place[1:2]).astype(BF16)
        turned = bv[2 * q:2 * q + 2, :ns].reshape(128, 128).T
        turned = jnp.concatenate([turned[:rows], turned[rows:]], axis=1)
        masks = (iota((ny, 256), 0) == place[0:1]).astype(BF16)
        masked = jnp.concatenate([turned * masks[b:b + 1] for b in range(ny)], axis=0)
        got = nt(masked, spread).reshape(ny, rows, 128)
        mv[...] = got if q == 0 else mv[...] + got

    keep = 1.0 - harvest
    zero = jnp.zeros((8, 128), F32)

    def block(lb, carry):
        sums, gone = carry
        cols = pl.ds(pl.multiple_of(lb * 128, 128), 128)
        new_sums, new_gone = [], []
        for il in range(il_n):
            tot, na, stay = zero, zero, zero
            for j in range(TYPES):
                m = jnp.broadcast_to(mv[lb, il * TYPES + j:il * TYPES + j + 1, :], (8, 128))
                term = m * stock[j, :, cols]
                tot = tot + term
                if j % il_n == il:
                    stay = jnp.where(x == j // il_n, term, stay)
                na = na + m * jnp.broadcast_to(areav[j:j + 1, cols], (8, 128))
            moved = tot - stay
            ns_i = stay + keep * moved
            new_sums.append(sums[il] + ns_i)
            new_gone.append(gone[il] + harvest * moved)
            snd[:, il, cols] = ns_i / na
            snd_a[il:il + 1, cols] = na[0:1]
        return tuple(new_sums), tuple(new_gone)

    zeros = (zero,) * il_n
    sums, gone = lax.fori_loop(0, ny, block, (zeros, zeros))

    word = zero
    for il in range(il_n):
        word = jnp.where(lane8 == row8 * il_n + il, jnp.sum(sums[il], axis=1, keepdims=True), word)
        word = jnp.where(lane8 == 8 * il_n + il, jnp.sum(gone[il], axis=1, keepdims=True), word)
    word = jnp.sum(word, axis=0, keepdims=True)
    red0[...] = word
    rc = []
    for o in far_s[::-1]:
        t, to = dev_s(o)
        rc.append(send(red0, red1.at[me], r1_s.at[o], r1_r.at[o], to))
    red1[pl.ds(me, 1)] = word.reshape(1, 1, 128)
    ocp = []
    for o in far_x:
        t, to = dev_x(o)
        ocp.append(send(snd_a, rcv_a.at[x], a_s.at[o], a_r.at[o], to))
        ocp.append(send(snd.at[pl.ds(2 * t, 2)], rcv.at[x], o_s.at[o], o_r.at[o], to))

    rcv[pl.ds(x, 1)] = snd[pl.ds(2 * x, 2)].reshape(1, 2, il_n, owned)
    rcv_a[pl.ds(x, 1)] = snd_a[...].reshape(1, il_n, owned)
    for cp in rc:
        cp.wait_recv()
    tot = red1[0]
    for s in range(1, ns):
        tot = tot + red1[s]
    red2[...] = tot
    rc = []
    for o in far_yx[::-1]:
        to = dev_yx(o)
        rc.append(send(red2, red3.at[y * nx + x], r2_s.at[o], r2_r.at[o], to))
    red3[pl.ds(y * nx + x, 1)] = tot.reshape(1, 1, 128)

    for cp in ocp:
        cp.wait_recv()
    run = None
    for i in range(TYPES):
        xs, il = i // il_n, i % il_n
        r = rcv_a[xs, il:il + 1, :]
        run = r if run is None else run + r
        out_cum[i:i + 1, :] = run
        for q in range(2):
            out_dens[q, i:i + 1, :] = rcv[xs, q, il:il + 1, :]
    out_cum[...] = out_cum[...] / run

    for cp in rc:
        cp.wait_recv()
    lane1 = iota((1, 128), 1)
    mean = [jnp.zeros((1, 128), F32)] * 2
    rem = jnp.zeros((1, 128), F32)
    for xs in range(nx):
        tot = red3[xs]
        for s in range(1, ny):
            tot = tot + red3[s * nx + xs]
        tot = tot / cells
        here = lane1 // il_n == xs
        rem = jnp.where(here, pltpu.roll(tot, 128 - 8 * il_n + xs * il_n, 1), rem)
        for q in range(2):
            away = lax.rem(128 + (xs - q) * il_n - 2 * il_n * x, 128)
            mean[q] = jnp.where(here, pltpu.roll(tot, away, 1), mean[q])
    out_rem[...] = rem[:, :TYPES]
    for q in range(2):
        out_mean[q:q + 1, :] = mean[q][:, :TYPES]
    for cp in sends:
        cp.wait_send()


def solution(mesh):
    nx = mesh.shape["pool"]
    nc = 2
    ncell = mesh.shape["cell"]
    nz = ny = int(round((ncell // nc) ** 0.5))
    finer = Mesh(mesh.devices.reshape(nz, ny, nc, nx), ("z", "y", "core", "pool"))
    ns = nz * nc
    half_n = 64 // ns
    owned = 128 * ny
    rows = 256 // nx
    il_n = TYPES // nx
    groups = ns * ny
    dims = (nz, ny, nc, nx, float(ncell * owned))
    any_, vm = pl.BlockSpec(memory_space=pl.ANY), pl.BlockSpec(memory_space=pltpu.VMEM)
    hbm = pl.BlockSpec(memory_space=pltpu.HBM)
    dma = pltpu.SemaphoreType.DMA

    def body(fractions, order, density, area, harvest):
        scratch = [
            pltpu.VMEM((2 * rows, owned), BF16),
            pltpu.VMEM((ny, 128), I32),
            pltpu.VMEM((TYPES, owned), F32),
            pltpu.SMEM((2,), F32),
            pltpu.VMEM((8, 128), F32),
            pltpu.VMEM((nx, 8, 128), F32),
            pltpu.VMEM((2 * nx, TYPES, owned), F32),
            pltpu.VMEM((TYPES, 2 * nx, owned), F32),
            pltpu.VMEM((ns, ny + 1, half_n, 128), BF16),
            pltpu.VMEM((ny + 1, ns + 1, half_n, 128), BF16),
            pltpu.VMEM((ny, ns + 1, half_n, 128), BF16),
            pltpu.VMEM((ny, rows, 128), F32),
            pltpu.VMEM((2 * nx, il_n, owned), F32),
            pltpu.VMEM((il_n, owned), F32),
            pltpu.VMEM((nx, 2, il_n, owned), F32),
            pltpu.VMEM((nx, il_n, owned), F32),
            pltpu.VMEM((1, 128), F32),
            pltpu.VMEM((ns, 1, 128), F32),
            pltpu.VMEM((1, 128), F32),
            pltpu.VMEM((ny * nx, 1, 128), F32),
            dma((6,)),
        ]
        for n in (nx, nx, ns, ny, ny, nx, nx, ns, ny * nx):
            scratch += [dma((n,)), dma((n,))]
        results = pl.pallas_call(
            functools.partial(kernel, dims),
            out_shape=(
                jax.ShapeDtypeStruct((2, TYPES, owned), F32),
                jax.ShapeDtypeStruct((TYPES, owned), F32),
                jax.ShapeDtypeStruct((2, TYPES), F32),
                jax.ShapeDtypeStruct((1, TYPES), F32),
            ),
            in_specs=[hbm] * 5,
            out_specs=(vm, vm, vm, vm),
            scratch_shapes=scratch,
            compiler_params=pltpu.CompilerParams(collective_id=0, has_side_effects=True, vmem_limit_bytes=VMEM_LIMIT),
        )(*(pltpu.with_memory_space_constraint(a, pltpu.HBM) for a in (fractions, order.reshape(ny, 128), density, area, harvest)))
        dens, cum, mean, rem = pl.pallas_call(
            hand_over,
            out_shape=tuple(jax.ShapeDtypeStruct(r.shape, r.dtype) for r in results),
            in_specs=[any_] * 4,
            out_specs=(hbm,) * 4,
            scratch_shapes=[dma((4,))],
            compiler_params=pltpu.CompilerParams(vmem_limit_bytes=VMEM_LIMIT),
        )(*results)
        return dens, cum, mean, rem.reshape(TYPES)

    cell = ("z", "y", "core")
    return jax.shard_map(
        body,
        mesh=finer,
        in_specs=(P(None, cell), P(cell), P("pool", None, cell), P(None, cell), P("pool")),
        out_specs=(P("pool", None, cell), P(None, cell), P("pool", None), P()),
        check_vma=False,
    )
```
